128 devices in a mesh: ep: 64 (over x_lo, z, y, core), tp: 2 (over x_hi).
Axes of the slice: x: 4 (x_hi: 2, x_lo: 2; x = x_hi * 2 + x_lo), y: 4, z: 4, core: 2. Of those that a mesh axis runs over, the one named last changes fastest.
Arguments:
- tokens: bfloat16 [8192, 2048], P('ep'), may hold values from -6 to 6
- expert_ids: int32 [8192, 8], P('ep'), may hold values from 0 to 127, all different within a row; in each aligned block of 128 rows (0 to 127, 128 to 255, ...) at most 12 rows name the same one
- combine: float32 [8192, 8], P('ep'), may hold values from 0.05 to 0.5
- cotangent: bfloat16 [8192, 2048], P('ep'), may hold values from -6 to 6
- old_layout: int32 [128], replicated, may hold values from 0 to 127, each once
- pair_moves: int32 [64], replicated, may hold values from 0 to 1, as said below
- gate_w: bfloat16 [128, 2048, 768], P('ep', None, 'tp'), may hold values from -0.125 to 0.125
- up_w: bfloat16 [128, 2048, 768], P('ep', None, 'tp'), may hold values from -0.125 to 0.125
- down_w: bfloat16 [128, 768, 2048], P('ep', 'tp'), may hold values from -0.21875 to 0.21875
Outputs:
- mixed: bfloat16 [8192, 2048], P('ep', 'tp')
- d_tokens: bfloat16 [8192, 2048], P('ep', 'tp')
- d_combine: float32 [8192, 8], P('ep')
- grad_gate: bfloat16 [128, 2048, 768], P('ep', None, 'tp')
- grad_up: bfloat16 [128, 2048, 768], P('ep', None, 'tp')
- grad_down: bfloat16 [128, 768, 2048], P('ep', 'tp')
The draws below stay inside these ranges and needn't reach their ends.
Inputs may be any that keep to these rules, and one draw needn't show every extreme that they name: `expert_ids`: among the 128 tokens of one ep index no expert is named more than 12 times, a bound that some block reaches. `old_layout`: A permutation of the experts. pair_moves[q] = pair_moves[q + 32]; at least one pair moves.
All inputs are finite; a program needn't handle non-finite values.
Results may differ from the reference program's by a relative error of at most 0.008.
Values may be sent and summed in bfloat16 or wider, within the bound.
A program may use at most 192 MiB of HBM per device.

```python
import math
import jax
import jax.numpy as jnp
import numpy as np
from jax import lax

D = 2048
FF = 768
TOP = 8
EXP_DEV = 2
TOK_DEV = 128
EXPERTS = 128
PAIRS = 32
CAP = 12
TOKENS = 8192
N_EP = 64


def draw_pair_moves(key, part):
    lower = jax.random.randint(key, (PAIRS,), 0, 2)
    chosen = jax.random.randint(jax.random.fold_in(key, 7), (), 0, PAIRS)
    lower = jnp.where(jnp.arange(PAIRS) == chosen, 1, lower)
    return jnp.concatenate([lower, lower]).astype(jnp.int32)


def block_scale(rng, dims, pieces, low, high):
    gain = 1.0
    for axis_at, parts in pieces:
        steps = jax.random.uniform(jax.random.fold_in(jax.random.fold_in(rng, 6), axis_at), (parts,), jnp.float32, low / len(pieces), high / len(pieces))
        gain = gain * jnp.repeat(jnp.exp(steps), dims[axis_at] // parts).reshape((-1,) + (1,) * (len(dims) - 1 - axis_at))
    return gain


def assign_block(key, own, number, rows, count, top, limit, slope):
    order = jax.random.permutation(key, count)
    packed, ordinary = portions_of(count, rows * top, limit, slope, True), portions_of(count, rows * top, limit, slope, False)
    places = jnp.arange(count)

    def named(sizes, offset_by):
        used = int((sizes > 0).sum())
        fixed = max(1, used // 4)
        shifted = fixed + (places - fixed + offset_by * (used - fixed)) % max(1, count - fixed)
        return jnp.zeros((count,), jnp.int32).at[order[jnp.where(places < fixed, places, shifted)]].set(jnp.asarray(sizes, jnp.int32))

    sizes = jnp.where(number % 4 == 0, named(packed, number // 4), named(ordinary, number - number // 4 - 1))
    mixed = jax.random.permutation(jax.random.fold_in(own, 3), count)
    giver, sink = mixed[0:count // 2 * 2:2], mixed[1:count // 2 * 2:2]
    margin = jnp.minimum(sizes[giver] - 1, limit - sizes[sink]) // 2
    margin = jnp.where((giver == order[0]) | (sink == order[0]) | (sizes[sink] == 0), 0, jnp.maximum(margin, 0))
    shifted = jax.random.randint(jax.random.fold_in(own, 4), (count // 2,), 0, 1 << 20) % (margin + 1)
    sizes = sizes.at[giver].add(-shifted).at[sink].add(shifted)
    items = jnp.searchsorted(jnp.cumsum(sizes), jnp.arange(rows * top), side="right").astype(jnp.int32)
    table = items.reshape(top, rows).T
    table = table[jax.random.permutation(jax.random.fold_in(own, 1), rows)]
    offset_by = jax.random.randint(jax.random.fold_in(own, 2), (rows, 1), 0, top)
    return jnp.take_along_axis(table, (jnp.arange(top)[None, :] + offset_by) % top, axis=1)


def portions_of(number_of, total, reach, skew, full):
    portions = [(1 << 20) // math.isqrt(rank ** skew) + 1 for rank in range(1, number_of + 1)]
    largest = reach if full else min(reach, max(-(-total // number_of), total * portions[0] // sum(portions)))
    least = 1 if total - largest >= number_of - 1 else 0
    counts, surplus = [largest] + [least] * (number_of - 1), total - largest - least * (number_of - 1)
    while surplus > 0:
        candidates = [i for i in range(1, number_of) if counts[i] < largest] or [i for i in range(1, number_of) if counts[i] < reach]
        whole, left = sum([portions[i] for i in candidates]), surplus
        for i in candidates:
            extra = min(reach - counts[i], max(1, left * portions[i] // whole), surplus)
            counts[i] = counts[i] + extra
            surplus = surplus - extra
    return np.array(counts)


def bell_draw(own_key, shape, deviation, bound, shards=(), kind=jnp.bfloat16):
    gain = block_scale(own_key, shape, shards, -0.22, 0.18) if shards else 1.0
    values = jax.random.normal(own_key, shape, jnp.float32) * deviation * gain
    return jnp.minimum(jnp.maximum(values, -bound), bound).astype(kind)


def setup_inputs(seed: int = 0) -> dict:
    key_of = jax.random.split(jax.random.key(seed), 10)
    tokens = bell_draw(key_of[0], (TOKENS, D), 1.0, 6.0, ((0, 64),))
    expert_ids_keys = jax.random.split(jax.random.fold_in(key_of[1], 1), TOKENS // TOK_DEV)
    expert_ids_turns = jax.random.permutation(jax.random.fold_in(key_of[1], 3), TOKENS // TOK_DEV)
    expert_ids = jax.vmap(lambda own, number: assign_block(jax.random.fold_in(key_of[1], 2), own, number, TOK_DEV, EXPERTS, TOP, CAP, 2))(expert_ids_keys, expert_ids_turns).reshape((TOKENS, TOP))
    combine = jnp.clip(jnp.exp(math.log(0.5) - 2.3025851 * jax.random.uniform(key_of[2], (TOKENS, TOP), jnp.float32) ** block_scale(key_of[2], (TOKENS, TOP), ((0, 64),), -0.2, 0.2)), 0.05, 0.5)
    cotangent = bell_draw(key_of[3], (TOKENS, D), 1.0, 6.0, ((0, 64),))
    old_layout = jax.random.permutation(key_of[4], EXPERTS).astype(jnp.int32)
    pair_moves = draw_pair_moves(jax.random.fold_in(key_of[9], 71), 0)
    gate_w = bell_draw(key_of[6], (EXPERTS, D, FF), D ** -0.5, 0.125, ((0, 64), (2, 2)))
    up_w = bell_draw(key_of[7], (EXPERTS, D, FF), D ** -0.5, 0.125, ((0, 64), (2, 2)))
    down_w = bell_draw(key_of[8], (EXPERTS, FF, D), FF ** -0.5, 0.21875, ((0, 64), (1, 2)))
    return {"tokens": tokens, "expert_ids": expert_ids, "combine": combine, "cotangent": cotangent, "old_layout": old_layout, "pair_moves": pair_moves, "gate_w": gate_w, "up_w": up_w, "down_w": down_w}


def expert_pass(rows_in, rows_grad, w_gate, w_up, w_down):
    gate = jnp.dot(rows_in, w_gate, preferred_element_type=jnp.float32)
    upper = jnp.dot(rows_in, w_up, preferred_element_type=jnp.float32)
    sigma = jax.nn.sigmoid(gate)
    active = gate * sigma
    hidden = (active * upper).astype(jnp.bfloat16)
    result = jnp.dot(hidden, w_down, preferred_element_type=jnp.float32).astype(jnp.bfloat16)
    d_hidden = jnp.dot(rows_grad, w_down.T, preferred_element_type=jnp.float32)
    d_gate = (d_hidden * upper * sigma * (1.0 + gate * (1.0 - sigma))).astype(jnp.bfloat16)
    d_up = (d_hidden * active).astype(jnp.bfloat16)
    d_rows = (jnp.dot(d_gate, w_gate.T, preferred_element_type=jnp.float32)
              + jnp.dot(d_up, w_up.T, preferred_element_type=jnp.float32)).astype(jnp.bfloat16)
    g_gate = jnp.dot(rows_in.T, d_gate, preferred_element_type=jnp.float32).astype(jnp.bfloat16)
    g_up = jnp.dot(rows_in.T, d_up, preferred_element_type=jnp.float32).astype(jnp.bfloat16)
    g_down = jnp.dot(hidden.T, rows_grad, preferred_element_type=jnp.float32).astype(jnp.bfloat16)
    return result, d_rows, g_gate, g_up, g_down


def reference(tokens, expert_ids, combine, cotangent, old_layout, pair_moves, gate_w, up_w, down_w):
    slot_ids = jnp.arange(EXPERTS, dtype=jnp.int32)
    slot_device = slot_ids // EXP_DEV
    slot_local = slot_ids % EXP_DEV
    moved = (slot_local == EXP_DEV - 1) & (pair_moves[slot_device] == 1)
    source_slot = jnp.where(moved, ((slot_device + PAIRS) % N_EP) * EXP_DEV + slot_local, slot_ids).astype(jnp.int32)
    new_layout = old_layout[source_slot]
    old_slot = jnp.zeros((EXPERTS,), jnp.int32).at[old_layout].set(slot_ids)
    blocks = expert_ids.reshape(N_EP, TOK_DEV * TOP)
    onehot = (blocks[..., None] == slot_ids[None, None, :]).astype(jnp.int32)
    before = jnp.cumsum(onehot, axis=1) - onehot
    position = jnp.sum(before * onehot, axis=-1).reshape(-1).astype(jnp.int32)
    flat_index = jnp.arange(TOKENS * TOP, dtype=jnp.int32)
    source_block = flat_index // (TOK_DEV * TOP)
    row_index = (source_block * CAP + position).astype(jnp.int32)
    token_of = flat_index // TOP
    expert_of = expert_ids.reshape(-1)
    rows_in = jnp.zeros((EXPERTS, N_EP * CAP, D), jnp.bfloat16).at[expert_of, row_index].set(tokens[token_of])
    grad_vals = (combine.reshape(-1)[:, None] * cotangent[token_of].astype(jnp.float32)).astype(jnp.bfloat16)
    rows_grad = jnp.zeros((EXPERTS, N_EP * CAP, D), jnp.bfloat16).at[expert_of, row_index].set(grad_vals)

    def one_expert(inputs):
        expert, x_rows, g_rows = inputs
        slot = old_slot[expert]
        return expert_pass(x_rows, g_rows, gate_w[slot], up_w[slot], down_w[slot])

    outputs, d_rows, g_gate, g_up, g_down = lax.map(one_expert, (slot_ids, rows_in, rows_grad))
    picked = outputs[expert_of, row_index].reshape(TOKENS, TOP, D)
    picked_grad = d_rows[expert_of, row_index].reshape(TOKENS, TOP, D)
    cot_float = cotangent.astype(jnp.float32)
    mixed = jnp.zeros((TOKENS, D), jnp.float32)
    d_tokens = jnp.zeros((TOKENS, D), jnp.float32)
    columns = []
    for choice_k in range(TOP):
        value_k = picked[:, choice_k].astype(jnp.float32)
        mixed = mixed + combine[:, choice_k][:, None] * value_k
        d_tokens = d_tokens + picked_grad[:, choice_k].astype(jnp.float32)
        columns.append(jnp.sum(cot_float * value_k, axis=-1))
    d_combine = jnp.stack(columns, axis=1)
    return (mixed.astype(jnp.bfloat16), d_tokens.astype(jnp.bfloat16), d_combine,
            g_gate[new_layout], g_up[new_layout], g_down[new_layout])
```

```python
import jax
import jax.numpy as jnp
from jax import lax
from jax.experimental import pallas as pl
from jax.experimental.pallas import tpu as pltpu
from jax.sharding import Mesh, PartitionSpec as P

MESH = pl.DeviceIdType.MESH
BF, F32 = jnp.bfloat16, jnp.float32
D, FF, CAP, TOK, TOP = 2048, 384, 12, 128, 8
META = 128
WIDE = D + META
BLOCKS = 8
ROWS = BLOCKS * CAP
ALL = BLOCKS * ROWS
HALF = D // 2
LIMIT = 66 * 1024 * 1024 - 4096
EP = ("xlo", "z", "y", "c")
ANY = pl.BlockSpec(memory_space=pl.ANY)
VMEM = pl.BlockSpec(memory_space=pltpu.VMEM)


def position():
    return {name: lax.axis_index(name) for name in ("xlo", "z", "y", "c", "xhi")}


def greet(devices):
    barrier = pltpu.get_barrier_semaphore()
    for device in devices:
        pl.semaphore_signal(barrier, inc=1, device_id=device, device_id_type=MESH)
    pl.semaphore_wait(barrier, len(devices))


def remote(source, target, send, recv, device):
    return pltpu.make_async_remote_copy(
        src_ref=source,
        dst_ref=target,
        send_sem=send,
        recv_sem=recv,
        device_id=device,
        device_id_type=MESH,
    )


def others(axis, me):
    found = []
    for step in range(1, 8):
        j = lax.rem(me + step, 8)
        found.append({axis: j // 2, "c": lax.rem(j, 2)})
    return found


def dispatch_kernel(
    tok_ref, cot_ref, e_tok, e_cot, wg, wu, wd,
    x_out, dy_out, st_tok_out, st_cot_out, wg_out, wu_out, wd_out,
    g_tok, g_cot, sel_tok, sel_cot, st_tok, st_cot, code_tok, code_cot, rowcode, upper,
    ag_send, ag_recv, x_send, x_recv, st_sem, loc_sem, w_send, w_recv,
):
    at = position()
    xlo, y, z, c, xhi = at["xlo"], at["y"], at["z"], at["c"], at["xhi"]
    direct, flipped = {"xlo": 1 - xlo}, {"xlo": 1 - xlo, "xhi": 1 - xhi}
    me_z, me_y = z * 2 + c, y * 2 + c
    greet([direct, flipped] + others("z", me_z) + others("y", me_y))

    paths = ((tok_ref, g_tok, "y", y, 0), (cot_ref, g_cot, "z", z, 1))

    def copies(source, gathered, axis, a, p):
        right, left = {axis: lax.rem(a + 1, 4)}, {axis: lax.rem(a + 3, 4)}
        opposite = lax.rem(a + 2, 4)
        mine, theirs = xlo * 4, (1 - xlo) * 4
        l, r = lax.rem(a + 3, 4), lax.rem(a + 1, 4)
        lo, hi = pl.ds(0, 64), pl.ds(64, 64)
        own = gathered.at[mine + a]
        plan = [
            (source, own, flipped, gathered.at[theirs + a]),
            (source, own, right, gathered.at[mine + l]),
            (source, own, left, gathered.at[mine + r]),
            (gathered.at[theirs + a], gathered.at[theirs + a], right, gathered.at[theirs + l]),
            (gathered.at[theirs + a], gathered.at[theirs + a], left, gathered.at[theirs + r]),
            (gathered.at[mine + l, lo], gathered.at[mine + l, lo], right, gathered.at[mine + opposite, lo]),
            (gathered.at[theirs + l, lo], gathered.at[theirs + l, lo], right, gathered.at[theirs + opposite, lo]),
            (gathered.at[mine + r, hi], gathered.at[mine + r, hi], left, gathered.at[mine + opposite, hi]),
            (gathered.at[theirs + r, hi], gathered.at[theirs + r, hi], left, gathered.at[theirs + opposite, hi]),
        ]
        out = [remote(s, t, ag_send.at[p, i], ag_recv.at[p, i], dev) for i, (s, t, dev, _) in enumerate(plan)]
        come = [remote(s, got, ag_send.at[p, i], ag_recv.at[p, i], dev) for i, (s, _, dev, got) in enumerate(plan)]
        local = pltpu.make_async_copy(source, own, loc_sem.at[p])
        return out, come, local

    tok, cot = copies(*paths[0]), copies(*paths[1])
    for out, _, local in (tok, cot):
        for i in (1, 2, 0):
            out[i].start()
        local.start()
    weights = [
        remote(src.at[1], dst, w_send.at[i], w_recv.at[i], direct)
        for i, (src, dst) in enumerate(((wg, wg_out), (wu, wu_out), (wd, wd_out)))
    ]
    for copy in weights:
        copy.start()

    row = lax.broadcasted_iota(jnp.int32, (ROWS, BLOCKS * TOK), 0)
    col = lax.broadcasted_iota(jnp.int32, (ROWS, BLOCKS * TOK), 1)
    value = jnp.full((ROWS, BLOCKS * TOK), -2, jnp.int32)
    for b in range(BLOCKS):
        inside = (row >= b * CAP) & (row < (b + 1) * CAP) & (col >= b * TOK) & (col < (b + 1) * TOK)
        value = jnp.where(inside, row - b * CAP, value)
    rowcode[...] = value.astype(F32)
    before = lax.broadcasted_iota(jnp.int32, (TOK, TOK), 0) < lax.broadcasted_iota(jnp.int32, (TOK, TOK), 1)
    upper[...] = jnp.where(before, 1.0, 0.0).astype(BF)

    for arrival, starts in ((0, (3, 4)), (1, (5,)), (2, (7,)), (3, (6,)), (4, (8,))):
        for out, come, _ in (tok, cot):
            come[arrival].wait_recv()
            for i in starts:
                out[i].start()
    for out, come, local in (tok, cot):
        for i in (5, 6, 7, 8):
            come[i].wait_recv()
        local.wait()

    for gathered, experts, code in ((g_tok, e_tok, code_tok), (g_cot, e_cot, code_cot)):
        for b in range(BLOCKS):
            ids = gathered[b, :, D:WIDE].astype(F32).T[0:TOP]
            member = jnp.zeros((16, TOK), F32)
            for k in range(TOP):
                member = member + jnp.where(ids[k : k + 1] == experts[...], 1.0, 0.0)
            place = jnp.dot(member.astype(BF), upper[...], preferred_element_type=F32)
            found = jnp.where(member > 0.5, place, -1.0)
            for d in range(8):
                code[d, 0:2, b * TOK : (b + 1) * TOK] = found[2 * d : 2 * d + 2]

    def emit(d, gathered, code, sel, st, width):
        rows = code[d]
        chosen = jnp.concatenate(
            [jnp.where(rowcode[...] == rows[l : l + 1], 1.0, 0.0) for l in range(2)], axis=0
        )
        st[d] = chosen.T.astype(BF)
        pick = chosen.astype(BF)

        def piece(start, size):
            source = gathered[:, :, pl.ds(start, size)].reshape(BLOCKS * TOK, size)
            got = jnp.dot(pick, source, preferred_element_type=F32).astype(BF)
            sel[d, :, :, pl.ds(start, size)] = got.reshape(2, ROWS, size)

        def step(n, carry):
            piece(pl.multiple_of(n * 256, 256), 256)
            return carry

        lax.fori_loop(0, D // 256, step, 0)
        if width > D:
            piece(D, META)

    sides = (
        (0, g_tok, code_tok, sel_tok, st_tok, st_tok_out, x_out, "z", me_z, WIDE),
        (1, g_cot, code_cot, sel_cot, st_cot, st_cot_out, dy_out, "y", me_y, D),
    )

    def exchange(p, j, sel, target, axis, slot):
        return remote(
            sel.at[j], target.at[:, slot], x_send.at[p, j], x_recv.at[p, slot],
            {axis: j // 2, "c": lax.rem(j, 2)},
        )

    def send(i, carry):
        for p, gathered, code, sel, st, st_out, target, axis, me, width in sides:
            d = lax.rem(me + i, 8)
            emit(d, gathered, code, sel, st, width)
            exchange(p, d, sel, target, axis, me).start()
            pltpu.make_async_copy(st.at[d], st_out.at[d], st_sem.at[p, d]).start()
        return carry

    lax.fori_loop(1, 8, send, 0)
    for p, gathered, code, sel, st, st_out, target, axis, me, width in sides:
        emit(me, gathered, code, sel, st, width)
        pltpu.make_async_copy(sel.at[me], target.at[:, me], loc_sem.at[2 + p]).start()
        pltpu.make_async_copy(st.at[me], st_out.at[me], st_sem.at[p, me]).start()

    def finish(i, carry):
        for p, gathered, code, sel, st, st_out, target, axis, me, width in sides:
            j = lax.rem(me + i, 8)
            exchange(p, j, sel, target, axis, j).wait_send()
            exchange(p, j, sel, target, axis, j).wait_recv()
            pltpu.make_async_copy(st.at[j], st_out.at[j], st_sem.at[p, j]).wait()
        return carry

    lax.fori_loop(1, 8, finish, 0)
    for p, gathered, code, sel, st, st_out, target, axis, me, width in sides:
        pltpu.make_async_copy(sel.at[me], target.at[:, me], loc_sem.at[2 + p]).wait()
        pltpu.make_async_copy(st.at[me], st_out.at[me], st_sem.at[p, me]).wait()
    for out, _, _ in (tok, cot):
        for copy in out:
            copy.wait_send()
    for copy in weights:
        copy.wait()


def dispatch(tok, cot, e_tok, e_cot, wg, wu, wd):
    gathered = pltpu.VMEM((BLOCKS, TOK, WIDE), BF)
    choice = pltpu.VMEM((8, BLOCKS * TOK, 2 * ROWS), BF)
    code = pltpu.VMEM((8, 8, BLOCKS * TOK), F32)
    dma = pltpu.SemaphoreType.DMA
    return pl.pallas_call(
        dispatch_kernel,
        name="dispatch",
        out_shape=(
            jax.ShapeDtypeStruct((2, 8, ROWS, WIDE), BF),
            jax.ShapeDtypeStruct((2, 8, ROWS, D), BF),
            jax.ShapeDtypeStruct((8, BLOCKS * TOK, 2 * ROWS), BF),
            jax.ShapeDtypeStruct((8, BLOCKS * TOK, 2 * ROWS), BF),
            jax.ShapeDtypeStruct((D, FF), BF),
            jax.ShapeDtypeStruct((D, FF), BF),
            jax.ShapeDtypeStruct((FF, D), BF),
        ),
        in_specs=[ANY, ANY, VMEM, VMEM, ANY, ANY, ANY],
        out_specs=[ANY] * 7,
        scratch_shapes=[
            gathered, gathered,
            pltpu.VMEM((8, 2, ROWS, WIDE), BF), pltpu.VMEM((8, 2, ROWS, D), BF),
            choice, choice, code, code,
            pltpu.VMEM((ROWS, BLOCKS * TOK), F32), pltpu.VMEM((TOK, TOK), BF),
            dma((2, 9)), dma((2, 9)), dma((2, 8)), dma((2, 8)), dma((2, 8)), dma((4,)), dma((3,)), dma((3,)),
        ],
        compiler_params=pltpu.CompilerParams(
            collective_id=0, has_side_effects=True, vmem_limit_bytes=LIMIT
        ),
    )(tok, cot, e_tok, e_cot, wg, wu, wd)


def expert_kernel(
    facts, x, dy, perm, wg, wu, wd, wg_new, wu_new, wd_new,
    y, dx, gg, gu, gd,
    vg, vu, vd, gate, upper, dh_hi, dh_lo, hid, dgate, dup, hid_c, dgate_c, dup_c, sem,
):
    l = pl.program_id(0)
    moved = facts[0] == 1
    pairs = ((wg, wg_new, vg), (wu, wu_new, vu), (wd, wd_new, vd))

    @pl.when(l == 0)
    def _():
        for i, (old, new, held) in enumerate(pairs):
            pltpu.make_async_copy(old.at[0], held.at[0], sem.at[0, i]).start()
        for i, (old, new, held) in enumerate(pairs):

            @pl.when(moved)
            def _(new=new, held=held, i=i):
                pltpu.make_async_copy(new, held.at[1], sem.at[1, i]).start()

            @pl.when(jnp.logical_not(moved))
            def _(old=old, held=held, i=i):
                pltpu.make_async_copy(old.at[1], held.at[1], sem.at[1, i]).start()

    for i, (old, new, held) in enumerate(pairs):
        pltpu.make_async_copy(old.at[0], held.at[l], sem.at[l, i]).wait()
    expert = jnp.where(l == 0, facts[1], facts[2]).astype(F32)

    def nt(a, b):
        return lax.dot_general(a, b, (((1,), (1,)), ((), ())), preferred_element_type=F32)

    def tn(a, b):
        return lax.dot_general(a, b, (((0,), (0,)), ((), ())), preferred_element_type=F32)

    def nn(a, b):
        return jnp.dot(a, b, preferred_element_type=F32)

    def first(i, carry):
        rows = pl.ds(pl.multiple_of(i * 384, 384), 384)
        own = x[0, rows, 0:D]
        gate[rows] = nn(own, vg[l])
        upper[rows] = nn(own, vu[l])
        dh = nt(dy[0, rows], vd[l])
        high = dh.astype(BF)
        dh_hi[rows] = high
        dh_lo[rows] = (dh - high.astype(F32)).astype(BF)
        return carry

    lax.fori_loop(0, ALL // 384, first, 0)

    def second(i, carry):
        rows = pl.ds(pl.multiple_of(i * 192, 192), 192)
        order = perm[rows]
        dh = nn(order, dh_hi[...]) + nn(order, dh_lo[...])
        g, u = gate[rows], upper[rows]
        sigma = jax.nn.sigmoid(g)
        active = g * sigma
        hidden = active * u
        meta = x[0, rows, D:WIDE].astype(F32)
        lane = lax.broadcasted_iota(jnp.int32, meta.shape, 1)
        named = jnp.where((meta == expert) & (lane < TOP), 1.0, 0.0)
        weight = pltpu.roll(meta, META - 8, 1) + (
            pltpu.roll(meta, META - 16, 1) + pltpu.roll(meta, META - 24, 1)
        )
        w = jnp.sum(named * weight, axis=1, keepdims=True)
        dc = jnp.sum(hidden * dh, axis=1, keepdims=True)
        y[0, rows, D:WIDE] = (named * dc).astype(BF)
        hid[rows] = (hidden * w).astype(BF)
        dh = dh * w
        dgate[rows] = (dh * u * sigma * (1.0 + g * (1.0 - sigma))).astype(BF)
        dup[rows] = (dh * active).astype(BF)
        return carry

    lax.fori_loop(0, ALL // 192, second, 0)

    def third(i, carry):
        rows = pl.ds(pl.multiple_of(i * 192, 192), 192)
        order = perm[rows]
        y[0, rows, 0:D] = nn(hid[rows], vd[l]).astype(BF)
        a = nn(order, dgate[...]).astype(BF)
        b = nn(order, dup[...]).astype(BF)
        hid_c[rows] = nn(order, hid[...]).astype(BF)
        dx[0, rows] = (nt(a, vg[l]) + nt(b, vu[l])).astype(BF)
        return carry

    lax.fori_loop(0, ALL // 192, third, 0)

    def fourth(i, carry):
        cols = pl.ds(pl.multiple_of(i * 512, 512), 512)
        own = x[0, :, cols]
        gg[0, cols] = tn(own, dgate[...]).astype(BF)
        gu[0, cols] = tn(own, dup[...]).astype(BF)
        gd[0, :, cols] = tn(hid_c[...], dy[0, :, cols]).astype(BF)
        return carry

    lax.fori_loop(0, D // 512, fourth, 0)


def experts(facts, x, dy, perm, wg, wu, wd, wg_new, wu_new, wd_new):
    def block(*shape):
        return pl.BlockSpec((1, *shape), lambda l: (l,) + (0,) * len(shape))

    small = pltpu.VMEM((ALL, FF), BF)
    wide = pltpu.VMEM((ALL, FF), F32)
    return pl.pallas_call(
        expert_kernel,
        name="experts",
        grid=(2,),
        out_shape=(
            jax.ShapeDtypeStruct((2, ALL, WIDE), BF),
            jax.ShapeDtypeStruct((2, ALL, D), BF),
            jax.ShapeDtypeStruct((2, D, FF), BF),
            jax.ShapeDtypeStruct((2, D, FF), BF),
            jax.ShapeDtypeStruct((2, FF, D), BF),
        ),
        in_specs=[
            pl.BlockSpec(memory_space=pltpu.SMEM),
            block(ALL, WIDE), block(ALL, D),
            pl.BlockSpec((ALL, ALL), lambda l: (0, 0), pipeline_mode=pl.Buffered(1)),
            ANY, ANY, ANY, ANY, ANY, ANY,
        ],
        out_specs=[block(ALL, WIDE), block(ALL, D), block(D, FF), block(D, FF), block(FF, D)],
        scratch_shapes=[
            pltpu.VMEM((2, D, FF), BF), pltpu.VMEM((2, D, FF), BF), pltpu.VMEM((2, FF, D), BF),
            wide, wide, small, small, small, small, small, small, small, small,
            pltpu.SemaphoreType.DMA((2, 3)),
        ],
        compiler_params=pltpu.CompilerParams(
            dimension_semantics=("arbitrary",), vmem_limit_bytes=LIMIT
        ),
    )(facts, x, dy, perm, wg, wu, wd, wg_new, wu_new, wd_new)


def return_kernel(
    y_ref, dx_ref, st_tok, st_cot,
    mixed, d_tokens, d_combine,
    c_tok, c_cot, s_tok, s_cot, m_tok, m_cot, rx_tok, rx_cot, xs_tok, xs_cot, ra_tok, ra_cot,
    a_send, a_recv, x_send, x_recv, f_send, f_recv, loc_sem,
):
    at = position()
    xlo, y, z, c, xhi = at["xlo"], at["y"], at["z"], at["c"], at["xhi"]
    me_z, me_y = z * 2 + c, y * 2 + c
    flips = ((0, 1), (1, 0), (1, 1))
    near = []
    for fx, ft in flips:
        near.append((1 - xlo if fx else xlo, 1 - xhi if ft else xhi))
    greet([{"xlo": a, "xhi": b} for a, b in near] + others("z", me_z) + others("y", me_y))

    sides = (
        (0, y_ref, c_tok, st_tok, s_tok, m_tok, rx_tok, xs_tok, ra_tok, "z", me_z, "y", y, HALF + META),
        (1, dx_ref, c_cot, st_cot, s_cot, m_cot, rx_cot, xs_cot, ra_cot, "y", me_y, "z", z, HALF),
    )

    def exchange(p, source, held, axis, j, slot):
        return remote(
            source.at[:, j], held.at[slot], a_send.at[p, j], a_recv.at[p, slot],
            {axis: j // 2, "c": lax.rem(j, 2)},
        )

    def send(i, carry):
        for p, source, held, st, s, m, rx, xs, ra, axis, me, other, a, width in sides:
            exchange(p, source, held, axis, lax.rem(me + i, 8), me).start()
        return carry

    lax.fori_loop(1, 8, send, 0)
    for p, source, held, st, s, m, rx, xs, ra, axis, me, other, a, width in sides:
        pltpu.make_async_copy(source.at[:, me], held.at[me], loc_sem.at[p]).start()
        pltpu.make_async_copy(st, s, loc_sem.at[2 + p]).start()

    def spread(p, m, rx, k):
        a, b = near[k]
        return remote(m.at[a, b], rx.at[xlo * 2 + xhi], x_send.at[p, k], x_recv.at[p, k], {"xlo": a, "xhi": b})

    for p, source, held, st, s, m, rx, xs, ra, axis, me, other, a, width in sides:

        def arrive(i, carry):
            exchange(p, source, held, axis, lax.rem(me + i, 8), lax.rem(me + i, 8)).wait_recv()
            return carry

        lax.fori_loop(1, 8, arrive, 0)
        pltpu.make_async_copy(source.at[:, me], held.at[me], loc_sem.at[p]).wait()
        pltpu.make_async_copy(st, s, loc_sem.at[2 + p]).wait()

        def total(start, size):
            acc = jnp.zeros((BLOCKS * TOK, size), F32)
            for d in range(8):
                part = held[d, :, :, pl.ds(start, size)].reshape(2 * ROWS, size)
                acc = acc + jnp.dot(s[d], part, preferred_element_type=F32)
            return acc.astype(BF).reshape(2, 4, TOK, size)

        for t in range(2):

            def step(n, carry):
                got = total(pl.multiple_of(t * HALF + n * 256, 256), 256)
                cols = pl.ds(pl.multiple_of(n * 256, 256), 256)
                for b in range(2):
                    m[b, t, :, :, cols] = got[b]
                return carry

            lax.fori_loop(0, HALF // 256, step, 0)
        if width > HALF:
            got = total(D, META)
            for t in range(2):
                for b in range(2):
                    m[b, t, :, :, HALF:width] = got[b]
        for k in range(3):
            spread(p, m, rx, k).start()

    def fold(p, xs, ra, other, a, k, slot):
        to = lax.rem(a + k, 4)
        return remote(xs.at[to], ra.at[slot], f_send.at[p, k], f_recv.at[p, k], {other: to})

    for p, source, held, st, s, m, rx, xs, ra, axis, me, other, a, width in sides:
        for k in range(3):
            spread(p, m, rx, k).wait_recv()

        def add(i, carry):
            acc = m[xlo, xhi, i].astype(F32)
            for k in range(3):
                acc = acc + rx[near[k][0] * 2 + near[k][1], i].astype(F32)
            xs[i] = acc.astype(BF)
            return carry

        lax.fori_loop(0, 4, add, 0)
        for k in range(1, 4):
            fold(p, xs, ra, other, a, k, a).start()

    for p, source, held, st, s, m, rx, xs, ra, axis, me, other, a, width in sides:
        for k in range(1, 4):
            fold(p, xs, ra, other, a, k, a).wait_recv()
        acc = xs[a].astype(F32)
        for k in range(1, 4):
            acc = acc + ra[lax.rem(a + k, 4)].astype(F32)
        (mixed, d_tokens)[p][...] = acc[:, 0:HALF].astype(BF)
        if width > HALF:
            d_combine[...] = acc[:, HALF : HALF + TOP]
    for p, source, held, st, s, m, rx, xs, ra, axis, me, other, a, width in sides:

        def sent(i, carry):
            exchange(p, source, held, axis, lax.rem(me + i, 8), me).wait_send()
            return carry

        lax.fori_loop(1, 8, sent, 0)
        for k in range(3):
            spread(p, m, rx, k).wait_send()
            fold(p, xs, ra, other, a, k + 1, a).wait_send()


def give_back(y, dx, st_tok, st_cot):
    dma = pltpu.SemaphoreType.DMA
    choice = pltpu.VMEM((8, BLOCKS * TOK, 2 * ROWS), BF)
    wide = HALF + META

    def both(*shape):
        return [pltpu.VMEM((*shape, wide), BF), pltpu.VMEM((*shape, HALF), BF)]

    return pl.pallas_call(
        return_kernel,
        name="give_back",
        out_shape=(
            jax.ShapeDtypeStruct((TOK, HALF), BF),
            jax.ShapeDtypeStruct((TOK, HALF), BF),
            jax.ShapeDtypeStruct((TOK, TOP), F32),
        ),
        in_specs=[ANY] * 4,
        out_specs=[VMEM] * 3,
        scratch_shapes=[
            pltpu.VMEM((8, 2, ROWS, WIDE), BF), pltpu.VMEM((8, 2, ROWS, D), BF),
            choice, choice,
            *both(2, 2, 4, TOK), *both(4, 4, TOK), *both(4, TOK), *both(4, TOK),
            dma((2, 8)), dma((2, 8)), dma((2, 3)), dma((2, 3)), dma((2, 4)), dma((2, 4)), dma((4,)),
        ],
        compiler_params=pltpu.CompilerParams(
            collective_id=1, has_side_effects=True, vmem_limit_bytes=LIMIT
        ),
    )(y, dx, st_tok, st_cot)


def body(tokens, expert_ids, combine, cotangent, old_layout, pair_moves, gate_w, up_w, down_w):
    at = position()
    xlo, y, z, c = at["xlo"], at["y"], at["z"], at["c"]
    slots = jnp.arange(128, dtype=jnp.int32)
    owner, local = slots // 2, slots % 2
    moved = (local == 1) & (pair_moves[owner] == 1)
    source = jnp.where(moved, (owner + 32) % 64 * 2 + local, slots)
    new_layout = jnp.sum(jnp.where(source[:, None] == slots[None, :], old_layout[None, :], 0), axis=1)
    by_place = new_layout.reshape(2, 4, 4, 4)
    plane = lax.dynamic_index_in_dim(by_place, xlo, 0, False)
    at_y = lax.dynamic_index_in_dim(plane, y, 1, False)
    at_z = lax.dynamic_index_in_dim(plane, z, 0, False)
    own = lax.dynamic_slice(at_z.reshape(16), ((y * 2 + c) * 2,), (2,))
    device = ((xlo * 4 + z) * 4 + y) * 2 + c
    flag = lax.dynamic_slice(pair_moves, (device,), (1,))
    facts = jnp.concatenate([flag, own])
    e_tok = jnp.broadcast_to(at_y.reshape(16, 1), (16, TOK)).astype(F32)
    e_cot = jnp.broadcast_to(at_z.reshape(16, 1), (16, TOK)).astype(F32)

    high = lax.reduce_precision(combine, 8, 7)
    middle = lax.reduce_precision(combine - high, 8, 7)
    low = lax.reduce_precision(combine - high - middle, 8, 7)
    meta = jnp.concatenate(
        [expert_ids.astype(BF), high.astype(BF), middle.astype(BF), low.astype(BF), jnp.zeros((TOK, META - 32), BF)],
        axis=1,
    )
    tok = jnp.concatenate([tokens, meta], axis=1)
    cot = jnp.concatenate([cotangent, meta], axis=1)
    x, dy, st_tok, st_cot, wg_new, wu_new, wd_new = dispatch(tok, cot, e_tok, e_cot, gate_w, up_w, down_w)

    r = jnp.arange(ALL, dtype=jnp.int32)
    there = (r // CAP % 4 * 2 + r // ROWS % 2) * ROWS + (r // (4 * CAP) % 2 * 4 + r // (2 * ROWS)) * CAP + r % CAP
    perm = (there[:, None] == r[None, :]).astype(BF)
    y_rows, dx_rows, gg, gu, gd = experts(
        facts, x.reshape(2, ALL, WIDE), dy.reshape(2, ALL, D), perm,
        gate_w, up_w, down_w, wg_new, wu_new, wd_new,
    )
    mixed, d_tokens, d_combine = give_back(
        y_rows.reshape(2, 8, ROWS, WIDE), dx_rows.reshape(2, 8, ROWS, D), st_tok, st_cot
    )
    return mixed, d_tokens, d_combine, gg, gu, gd


def solution(mesh):
    fine = Mesh(mesh.devices.reshape(2, 4, 4, 2, 2), (*EP, "xhi"))
    return jax.shard_map(
        body,
        mesh=fine,
        in_specs=(
            P(EP, None), P(EP, None), P(EP, None), P(EP, None), P(), P(),
            P(EP, None, "xhi"), P(EP, None, "xhi"), P(EP, "xhi", None),
        ),
        out_specs=(
            P(EP, "xhi"), P(EP, "xhi"), P(EP, None),
            P(EP, None, "xhi"), P(EP, None, "xhi"), P(EP, "xhi", None),
        ),
        check_vma=False,
    )
```

```python
import jax
import jax.numpy as jnp
from jax import lax
from jax.experimental import pallas as pl
from jax.experimental.pallas import tpu as pltpu
from jax.sharding import Mesh, PartitionSpec as P

MESH = pl.DeviceIdType.MESH
BF, F32 = jnp.bfloat16, jnp.float32
D, FF, CAP, TOK, TOP = 2048, 384, 12, 128, 8
META = 128
WIDE = D + META
BLOCKS = 8
GROUP, SPAN = 4 * CAP, 4 * TOK
ROWS = BLOCKS * CAP
ALL = BLOCKS * ROWS
HALF = D // 2
Q = 4
PART = HALF // Q
LIMIT = 66 * 1024 * 1024 - 4096
EP = ("xlo", "z", "y", "c")
ANY = pl.BlockSpec(memory_space=pl.ANY)
VMEM = pl.BlockSpec(memory_space=pltpu.VMEM)


def position():
    return {name: lax.axis_index(name) for name in ("xlo", "z", "y", "c", "xhi")}


def greet(devices):
    barrier = pltpu.get_barrier_semaphore()
    for device in devices:
        pl.semaphore_signal(barrier, inc=1, device_id=device, device_id_type=MESH)
    pl.semaphore_wait(barrier, len(devices))


def remote(source, target, send, recv, device):
    return pltpu.make_async_remote_copy(
        src_ref=source,
        dst_ref=target,
        send_sem=send,
        recv_sem=recv,
        device_id=device,
        device_id_type=MESH,
    )


def others(axis, me):
    found = []
    for step in range(1, 8):
        j = lax.rem(me + step, 8)
        found.append({axis: j // 2, "c": lax.rem(j, 2)})
    return found


def dispatch_kernel(
    tok_ref, cot_ref, e_tok, e_cot, wg, wu, wd,
    x_out, dy_out, st_tok_out, st_cot_out, wg_out, wu_out, wd_out,
    g_tok, g_cot, sel_tok, sel_cot, st_tok, st_cot, code_tok, code_cot, rowcode, upper,
    ag_send, ag_recv, x_send, x_recv, st_sem, loc_sem, w_send, w_recv,
):
    at = position()
    xlo, y, z, c, xhi = at["xlo"], at["y"], at["z"], at["c"], at["xhi"]
    direct, flipped = {"xlo": 1 - xlo}, {"xlo": 1 - xlo, "xhi": 1 - xhi}
    me_z, me_y = z * 2 + c, y * 2 + c
    greet([direct, flipped] + others("z", me_z) + others("y", me_y))

    paths = ((tok_ref, g_tok, "y", y, 0), (cot_ref, g_cot, "z", z, 1))

    def copies(source, gathered, axis, a, p):
        right, left = {axis: lax.rem(a + 1, 4)}, {axis: lax.rem(a + 3, 4)}
        opposite = lax.rem(a + 2, 4)
        mine, theirs = xlo * 4, (1 - xlo) * 4
        l, r = lax.rem(a + 3, 4), lax.rem(a + 1, 4)
        lo, hi = pl.ds(0, 64), pl.ds(64, 64)
        own = gathered.at[mine + a]
        plan = [
            (source, own, flipped, gathered.at[theirs + a]),
            (source, own, right, gathered.at[mine + l]),
            (source, own, left, gathered.at[mine + r]),
            (gathered.at[theirs + a], gathered.at[theirs + a], right, gathered.at[theirs + l]),
            (gathered.at[theirs + a], gathered.at[theirs + a], left, gathered.at[theirs + r]),
            (gathered.at[mine + l, lo], gathered.at[mine + l, lo], right, gathered.at[mine + opposite, lo]),
            (gathered.at[theirs + l, lo], gathered.at[theirs + l, lo], right, gathered.at[theirs + opposite, lo]),
            (gathered.at[mine + r, hi], gathered.at[mine + r, hi], left, gathered.at[mine + opposite, hi]),
            (gathered.at[theirs + r, hi], gathered.at[theirs + r, hi], left, gathered.at[theirs + opposite, hi]),
        ]
        out = [remote(s, t, ag_send.at[p, i], ag_recv.at[p, i], dev) for i, (s, t, dev, _) in enumerate(plan)]
        come = [remote(s, got, ag_send.at[p, i], ag_recv.at[p, i], dev) for i, (s, _, dev, got) in enumerate(plan)]
        local = pltpu.make_async_copy(source, own, loc_sem.at[p])
        return out, come, local

    tok, cot = copies(*paths[0]), copies(*paths[1])
    for out, _, local in (tok, cot):
        for i in (1, 2, 0):
            out[i].start()
        local.start()
    weights = [
        remote(src.at[1], dst, w_send.at[i], w_recv.at[i], direct)
        for i, (src, dst) in enumerate(((wg, wg_out), (wu, wu_out), (wd, wd_out)))
    ]
    for copy in weights:
        copy.start()

    row = lax.broadcasted_iota(jnp.int32, (GROUP, SPAN), 0)
    col = lax.broadcasted_iota(jnp.int32, (GROUP, SPAN), 1)
    value = jnp.full((GROUP, SPAN), -2, jnp.int32)
    for b in range(4):
        inside = (row >= b * CAP) & (row < (b + 1) * CAP) & (col >= b * TOK) & (col < (b + 1) * TOK)
        value = jnp.where(inside, row - b * CAP, value)
    rowcode[...] = value.astype(F32)
    before = lax.broadcasted_iota(jnp.int32, (TOK, TOK), 0) < lax.broadcasted_iota(jnp.int32, (TOK, TOK), 1)
    upper[...] = jnp.where(before, 1.0, 0.0).astype(BF)

    for arrival, starts in ((0, (3, 4)), (1, (5,)), (2, (7,)), (3, (6,)), (4, (8,))):
        for out, come, _ in (tok, cot):
            come[arrival].wait_recv()
            for i in starts:
                out[i].start()
    for out, come, local in (tok, cot):
        for i in (5, 6, 7, 8):
            come[i].wait_recv()
        local.wait()

    def choose(gathered, experts, code, st):
        for b in range(BLOCKS):
            ids = gathered[b, :, D:WIDE].astype(F32).T[0:TOP]
            member = jnp.zeros((16, TOK), F32)
            for k in range(TOP):
                member = member + jnp.where(ids[k : k + 1] == experts[...], 1.0, 0.0)
            place = jnp.dot(member.astype(BF), upper[...], preferred_element_type=F32)
            found = jnp.where(member > 0.5, place, -1.0)
            for d in range(8):
                code[d, 0:2, b * TOK : (b + 1) * TOK] = found[2 * d : 2 * d + 2]

        def fill(d, carry):
            rows = code[d]
            for g in range(2):
                for l in range(2):
                    wanted = rows[l : l + 1, g * SPAN : (g + 1) * SPAN]
                    to = pl.ds(pl.multiple_of(d * 2 * GROUP + l * GROUP, GROUP), GROUP)
                    st[g, to] = jnp.where(rowcode[...] == wanted, 1.0, 0.0).astype(BF)
            return carry

        lax.fori_loop(0, 8, fill, 0)

    def emit(pair, gathered, sel, st, width):
        from_rows = pl.ds(pl.multiple_of(pair * 4 * GROUP, 4 * GROUP), 4 * GROUP)

        def piece(start, size):
            cols = pl.ds(start, size)
            for g in range(2):
                source = gathered[g * 4 : (g + 1) * 4, :, cols].reshape(SPAN, size)
                got = jnp.dot(st[g, from_rows], source, preferred_element_type=F32).astype(BF)
                sel[pl.ds(pair * 2, 2), :, g * GROUP : (g + 1) * GROUP, cols] = got.reshape(2, 2, GROUP, size)

        def step(n, carry):
            piece(pl.multiple_of(n * 512, 512), 512)
            return carry

        lax.fori_loop(0, D // 512, step, 0)
        if width > D:
            piece(D, META)

    sides = (
        (0, g_tok, e_tok, code_tok, sel_tok, st_tok, st_tok_out, x_out, "z", z, WIDE),
        (1, g_cot, e_cot, code_cot, sel_cot, st_cot, st_cot_out, dy_out, "y", y, D),
    )

    def exchange(p, j, sel, target, axis, slot):
        return remote(
            sel.at[j], target.at[:, slot], x_send.at[p, j], x_recv.at[p, slot],
            {axis: j // 2, "c": lax.rem(j, 2)},
        )

    for p, gathered, experts, code, sel, st, st_out, target, axis, b, width in sides:
        choose(gathered, experts, code, st)
        pltpu.make_async_copy(st, st_out, st_sem.at[p]).start()

    def send(i, carry):
        for p, gathered, experts, code, sel, st, st_out, target, axis, b, width in sides:
            pair = lax.rem(b + i, 4)
            emit(pair, gathered, sel, st, width)
            for core in range(2):
                exchange(p, pair * 2 + core, sel, target, axis, b * 2 + c).start()
        return carry

    lax.fori_loop(1, 4, send, 0)
    for p, gathered, experts, code, sel, st, st_out, target, axis, b, width in sides:
        emit(b, gathered, sel, st, width)
        exchange(p, b * 2 + 1 - c, sel, target, axis, b * 2 + c).start()
        pltpu.make_async_copy(sel.at[b * 2 + c], target.at[:, b * 2 + c], loc_sem.at[2 + p]).start()

    def finish(i, carry):
        for p, gathered, experts, code, sel, st, st_out, target, axis, b, width in sides:
            j = lax.rem(b * 2 + c + i, 8)
            exchange(p, j, sel, target, axis, j).wait_send()
            exchange(p, j, sel, target, axis, j).wait_recv()
        return carry

    lax.fori_loop(1, 8, finish, 0)
    for p, gathered, experts, code, sel, st, st_out, target, axis, b, width in sides:
        pltpu.make_async_copy(sel.at[b * 2 + c], target.at[:, b * 2 + c], loc_sem.at[2 + p]).wait()
        pltpu.make_async_copy(st, st_out, st_sem.at[p]).wait()
    for out, _, _ in (tok, cot):
        for copy in out:
            copy.wait_send()
    for copy in weights:
        copy.wait()


def dispatch(tok, cot, e_tok, e_cot, wg, wu, wd):
    gathered = pltpu.VMEM((BLOCKS, TOK, WIDE), BF)
    choice = pltpu.VMEM((2, ALL, SPAN), BF)
    code = pltpu.VMEM((8, 8, BLOCKS * TOK), F32)
    dma = pltpu.SemaphoreType.DMA
    return pl.pallas_call(
        dispatch_kernel,
        name="dispatch",
        out_shape=(
            jax.ShapeDtypeStruct((2, 8, ROWS, WIDE), BF),
            jax.ShapeDtypeStruct((2, 8, ROWS, D), BF),
            jax.ShapeDtypeStruct((2, ALL, SPAN), BF),
            jax.ShapeDtypeStruct((2, ALL, SPAN), BF),
            jax.ShapeDtypeStruct((D, FF), BF),
            jax.ShapeDtypeStruct((D, FF), BF),
            jax.ShapeDtypeStruct((FF, D), BF),
        ),
        in_specs=[ANY, ANY, VMEM, VMEM, ANY, ANY, ANY],
        out_specs=[ANY] * 7,
        scratch_shapes=[
            gathered, gathered,
            pltpu.VMEM((8, 2, ROWS, WIDE), BF), pltpu.VMEM((8, 2, ROWS, D), BF),
            choice, choice, code, code,
            pltpu.VMEM((GROUP, SPAN), F32), pltpu.VMEM((TOK, TOK), BF),
            dma((2, 9)), dma((2, 9)), dma((2, 8)), dma((2, 8)), dma((2,)), dma((4,)), dma((3,)), dma((3,)),
        ],
        compiler_params=pltpu.CompilerParams(
            collective_id=0, has_side_effects=True, vmem_limit_bytes=LIMIT
        ),
    )(tok, cot, e_tok, e_cot, wg, wu, wd)


def expert_kernel(
    facts, x, dy, perm, wg, wu, wd, wg_new, wu_new, wd_new,
    y, ym, dx, gg, gu, gd,
    vg, vu, vd, gate, upper, dh_hi, dh_lo, hid, dgate, dup, hid_c, dgate_c, dup_c, sem,
):
    l = pl.program_id(0)
    moved = facts[0] == 1
    pairs = ((wg, wg_new, vg), (wu, wu_new, vu), (wd, wd_new, vd))

    @pl.when(l == 0)
    def _():
        for i, (old, new, held) in enumerate(pairs):
            pltpu.make_async_copy(old.at[0], held.at[0], sem.at[0, i]).start()
        for i, (old, new, held) in enumerate(pairs):

            @pl.when(moved)
            def _(new=new, held=held, i=i):
                pltpu.make_async_copy(new, held.at[1], sem.at[1, i]).start()

            @pl.when(jnp.logical_not(moved))
            def _(old=old, held=held, i=i):
                pltpu.make_async_copy(old.at[1], held.at[1], sem.at[1, i]).start()

    for i, (old, new, held) in enumerate(pairs):
        pltpu.make_async_copy(old.at[0], held.at[l], sem.at[l, i]).wait()
    expert = jnp.where(l == 0, facts[1], facts[2]).astype(F32)

    def nt(a, b):
        return lax.dot_general(a, b, (((1,), (1,)), ((), ())), preferred_element_type=F32)

    def tn(a, b):
        return lax.dot_general(a, b, (((0,), (0,)), ((), ())), preferred_element_type=F32)

    def nn(a, b):
        return jnp.dot(a, b, preferred_element_type=F32)

    def first(i, carry):
        rows = pl.ds(pl.multiple_of(i * 384, 384), 384)
        own = x[0, rows, 0:D]
        gate[rows] = nn(own, vg[l])
        upper[rows] = nn(own, vu[l])
        dh = nt(dy[0, rows], vd[l])
        high = dh.astype(BF)
        dh_hi[rows] = high
        dh_lo[rows] = (dh - high.astype(F32)).astype(BF)
        return carry

    lax.fori_loop(0, ALL // 384, first, 0)

    def second(i, carry):
        rows = pl.ds(pl.multiple_of(i * 192, 192), 192)
        order = perm[rows]
        dh = nn(order, dh_hi[...]) + nn(order, dh_lo[...])
        g, u = gate[rows], upper[rows]
        sigma = jax.nn.sigmoid(g)
        active = g * sigma
        hidden = active * u
        meta = x[0, rows, D:WIDE].astype(F32)
        lane = lax.broadcasted_iota(jnp.int32, meta.shape, 1)
        named = jnp.where((meta == expert) & (lane < TOP), 1.0, 0.0)
        weight = pltpu.roll(meta, META - 8, 1) + (
            pltpu.roll(meta, META - 16, 1) + pltpu.roll(meta, META - 24, 1)
        )
        w = jnp.sum(named * weight, axis=1, keepdims=True)
        dc = jnp.sum(hidden * dh, axis=1, keepdims=True)
        ym[0, rows] = (named * dc).astype(BF)
        hid[rows] = (hidden * w).astype(BF)
        dh = dh * w
        dgate[rows] = (dh * u * sigma * (1.0 + g * (1.0 - sigma))).astype(BF)
        dup[rows] = (dh * active).astype(BF)
        return carry

    lax.fori_loop(0, ALL // 192, second, 0)

    def store(ref, rows, value):
        for q in range(Q):
            for t in range(2):
                start = t * HALF + q * PART
                ref[q, 0, rows, t * PART : (t + 1) * PART] = value[:, start : start + PART]

    def third(i, carry):
        rows = pl.ds(pl.multiple_of(i * 192, 192), 192)
        order = perm[rows]
        store(y, rows, nn(hid[rows], vd[l]).astype(BF))
        a = nn(order, dgate[...]).astype(BF)
        b = nn(order, dup[...]).astype(BF)
        hid_c[rows] = nn(order, hid[...]).astype(BF)
        store(dx, rows, (nt(a, vg[l]) + nt(b, vu[l])).astype(BF))
        return carry

    lax.fori_loop(0, ALL // 192, third, 0)

    def fourth(i, carry):
        cols = pl.ds(pl.multiple_of(i * 512, 512), 512)
        own = x[0, :, cols]
        gg[0, cols] = tn(own, dgate[...]).astype(BF)
        gu[0, cols] = tn(own, dup[...]).astype(BF)
        gd[0, :, cols] = tn(hid_c[...], dy[0, :, cols]).astype(BF)
        return carry

    lax.fori_loop(0, D // 512, fourth, 0)


def experts(facts, x, dy, perm, wg, wu, wd, wg_new, wu_new, wd_new):
    def block(*shape):
        return pl.BlockSpec((1, *shape), lambda l: (l,) + (0,) * len(shape))

    parts = pl.BlockSpec((Q, 1, ALL, 2 * PART), lambda l: (0, l, 0, 0))
    small = pltpu.VMEM((ALL, FF), BF)
    wide = pltpu.VMEM((ALL, FF), F32)
    return pl.pallas_call(
        expert_kernel,
        name="experts",
        grid=(2,),
        out_shape=(
            jax.ShapeDtypeStruct((Q, 2, ALL, 2 * PART), BF),
            jax.ShapeDtypeStruct((2, ALL, META), BF),
            jax.ShapeDtypeStruct((Q, 2, ALL, 2 * PART), BF),
            jax.ShapeDtypeStruct((2, D, FF), BF),
            jax.ShapeDtypeStruct((2, D, FF), BF),
            jax.ShapeDtypeStruct((2, FF, D), BF),
        ),
        in_specs=[
            pl.BlockSpec(memory_space=pltpu.SMEM),
            block(ALL, WIDE), block(ALL, D),
            pl.BlockSpec((ALL, ALL), lambda l: (0, 0), pipeline_mode=pl.Buffered(1)),
            ANY, ANY, ANY, ANY, ANY, ANY,
        ],
        out_specs=[parts, block(ALL, META), parts, block(D, FF), block(D, FF), block(FF, D)],
        scratch_shapes=[
            pltpu.VMEM((2, D, FF), BF), pltpu.VMEM((2, D, FF), BF), pltpu.VMEM((2, FF, D), BF),
            wide, wide, small, small, small, small, small, small, small, small,
            pltpu.SemaphoreType.DMA((2, 3)),
        ],
        compiler_params=pltpu.CompilerParams(
            dimension_semantics=("arbitrary",), vmem_limit_bytes=LIMIT
        ),
    )(facts, x, dy, perm, wg, wu, wd, wg_new, wu_new, wd_new)


def return_kernel(
    y_ref, ym_ref, dx_ref, st_tok, st_cot,
    mixed, d_tokens, d_combine,
    c_tok, c_meta, c_cot, raw_tok, raw_cot, s_tok, s_cot, m_tok, m_meta, m_cot,
    h_tok, h_meta, h_cot, rx_tok, rx_meta, rx_cot, xs_tok, xs_meta, xs_cot, ra_tok, ra_meta, ra_cot,
    a_send, a_recv, h_send, h_recv, x_send, x_recv, f_send, f_recv, loc_sem, st_sem,
):
    at = position()
    xlo, y, z, c, xhi = at["xlo"], at["y"], at["z"], at["c"], at["xhi"]
    near = ({"xlo": 1 - xlo}, {"xlo": 1 - xlo, "xhi": 1 - xhi})
    their_t = (xhi, 1 - xhi)
    greet([*near, *others("z", z * 2 + c), *others("y", y * 2 + c)])

    tok = (0, y_ref, c_tok, s_tok, m_tok, h_tok, rx_tok, xs_tok, ra_tok, "z", z * 2 + c, "y", y)
    cot = (1, dx_ref, c_cot, s_cot, m_cot, h_cot, rx_cot, xs_cot, ra_cot, "y", y * 2 + c, "z", z)
    small = (2, ym_ref, c_meta, s_tok, m_meta, h_meta, rx_meta, xs_meta, ra_meta, "z", z * 2 + c, "y", y)

    def exchange(side, q, j, slot):
        p, source, held, s, m, h, rx, xs, ra, axis, me, other, a = side
        return remote(
            source.at[q, :, j], held.at[q, slot], a_send.at[p, q, j], a_recv.at[p, q, slot],
            {axis: j // 2, "c": lax.rem(j, 2)},
        )

    def own(side, q):
        p, source, held, s, m, h, rx, xs, ra, axis, me, other, a = side
        return pltpu.make_async_copy(source.at[q, :, me], held.at[q, me], loc_sem.at[p, q])

    def relay(side, q, k):
        p, source, held, s, m, h, rx, xs, ra, axis, me, other, a = side
        piece = m.at[q, xlo, 0 if p == 2 else 1 - xhi, pl.ds(2 * k, 2)]
        return remote(piece, h.at[q, k], h_send.at[p, q, k], h_recv.at[p, q, k], near[k])

    def spread(side, q, k):
        p, source, held, s, m, h, rx, xs, ra, axis, me, other, a = side
        piece = m.at[q, 1 - xlo, k if p == 2 else their_t[k]]
        return remote(piece, rx.at[q, k], x_send.at[p, q, k], x_recv.at[p, q, k], near[k])

    def fold(side, q, k, slot):
        p, source, held, s, m, h, rx, xs, ra, axis, me, other, a = side
        to = lax.rem(a + k, 4)
        return remote(xs.at[q, to], ra.at[q, slot], f_send.at[p, q, k], f_recv.at[p, q, k], {other: to})

    def begin(side, q):
        def send(i, carry):
            exchange(side, q, lax.rem(side[10] + i, 8), side[10]).start()
            return carry

        lax.fori_loop(1, 8, send, 0)
        own(side, q).start()

    def begin_part(q, carry):
        begin(tok, q)
        begin(cot, q)
        return carry

    begin(small, 0)
    lax.fori_loop(0, Q, begin_part, 0)
    loads = [
        pltpu.make_async_copy(src, raw, st_sem.at[i]) for i, (src, raw) in enumerate(((st_tok, raw_tok), (st_cot, raw_cot)))
    ]
    for load in loads:
        load.start()
    for load, raw, s in ((loads[0], raw_tok, s_tok), (loads[1], raw_cot, s_cot)):
        load.wait()
        for g in range(2):

            def turn(n, carry, raw=raw, s=s, g=g):
                cols = pl.ds(pl.multiple_of(n * 128, 128), 128)
                s[g, cols] = raw[g, :, cols].astype(F32).T.astype(BF)
                return carry

            lax.fori_loop(0, SPAN // 128, turn, 0)

    def combine(side, q):
        p, source, held, s, m, h, rx, xs, ra, axis, me, other, a = side

        def arrive(i, carry):
            j = lax.rem(me + i, 8)
            exchange(side, q, j, j).wait_recv()
            return carry

        lax.fori_loop(1, 8, arrive, 0)
        own(side, q).wait()
        size = held.shape[-1]
        for g in range(2):
            part = held[q, :, :, g * GROUP : (g + 1) * GROUP].reshape(ALL, size)
            got = jnp.dot(s[g], part, preferred_element_type=F32).astype(BF)
            if p == 2:
                for t in range(2):
                    m[q, g, t] = got.reshape(4, TOK, META)
            else:
                for t in range(2):
                    m[q, g, t] = got[:, t * PART : (t + 1) * PART].reshape(4, TOK, PART)
        for k in range(2):
            relay(side, q, k).start()

    def pass_on(side, q):
        p, source, held, s, m, h, rx, xs, ra, axis, me, other, a = side
        for k in range(2):
            relay(side, q, k).wait_recv()
            t = (1 - k) if p == 2 else their_t[1 - k]
            half = pl.ds(2 * k, 2)
            total = m[q, 1 - xlo, t, half].astype(F32) + h[q, k].astype(F32)
            m[q, 1 - xlo, t, half] = total.astype(BF)
        for k in range(2):
            spread(side, q, k).start()

    def gather(side, q):
        p, source, held, s, m, h, rx, xs, ra, axis, me, other, a = side
        for k in range(2):
            spread(side, q, k).wait_recv()
        total = m[q, xlo, 0 if p == 2 else xhi].astype(F32)
        for k in range(2):
            total = total + rx[q, k].astype(F32)
        xs[q] = total.astype(BF)
        for k in range(1, 4):
            fold(side, q, k, a).start()

    def close(side, q):
        p, source, held, s, m, h, rx, xs, ra, axis, me, other, a = side
        for k in range(1, 4):
            fold(side, q, k, a).wait_recv()
        total = xs[q, a].astype(F32)
        for k in range(1, 4):
            total = total + ra[q, lax.rem(a + k, 4)].astype(F32)
        if p == 2:
            d_combine[...] = total[:, 0:TOP]
        else:
            (mixed, d_tokens)[p][:, pl.ds(pl.multiple_of(q * PART, PART), PART)] = total.astype(BF)
        for k in range(2):
            relay(side, q, k).wait_send()
            spread(side, q, k).wait_send()
            fold(side, q, k + 1, a).wait_send()
        fold(side, q, 3, a).wait_send()

        def sent(i, carry):
            exchange(side, q, lax.rem(me + i, 8), me).wait_send()
            return carry

        lax.fori_loop(1, 8, sent, 0)

    def both(stage, q):
        stage(tok, q)
        stage(cot, q)

    combine(small, 0)
    both(combine, 0)
    pass_on(small, 0)
    both(pass_on, 0)
    both(combine, 1)
    gather(small, 0)
    both(gather, 0)
    both(pass_on, 1)

    def flow(q, carry):
        both(combine, q)
        both(gather, q - 1)
        both(pass_on, q)
        both(close, q - 2)
        return carry

    lax.fori_loop(2, Q, flow, 0)
    close(small, 0)
    both(gather, Q - 1)
    both(close, Q - 2)
    both(close, Q - 1)


def give_back(y, ym, dx, st_tok, st_cot):
    dma = pltpu.SemaphoreType.DMA

    def each(*shape):
        return [
            pltpu.VMEM((Q, *shape, PART), BF), pltpu.VMEM((1, *shape, META), BF), pltpu.VMEM((Q, *shape, PART), BF)
        ]

    held = (8, 2, ROWS)
    return pl.pallas_call(
        return_kernel,
        name="give_back",
        out_shape=(
            jax.ShapeDtypeStruct((TOK, HALF), BF),
            jax.ShapeDtypeStruct((TOK, HALF), BF),
            jax.ShapeDtypeStruct((TOK, TOP), F32),
        ),
        in_specs=[ANY] * 5,
        out_specs=[VMEM] * 3,
        scratch_shapes=[
            pltpu.VMEM((Q, *held, 2 * PART), BF), pltpu.VMEM((1, *held, META), BF), pltpu.VMEM((Q, *held, 2 * PART), BF),
            pltpu.VMEM((2, ALL, SPAN), BF), pltpu.VMEM((2, ALL, SPAN), BF),
            pltpu.VMEM((2, SPAN, ALL), BF), pltpu.VMEM((2, SPAN, ALL), BF),
            *each(2, 2, 4, TOK), *each(2, 2, TOK), *each(2, 4, TOK), *each(4, TOK), *each(4, TOK),
            dma((3, Q, 8)), dma((3, Q, 8)), dma((3, Q, 2)), dma((3, Q, 2)), dma((3, Q, 2)), dma((3, Q, 2)),
            dma((3, Q, 4)), dma((3, Q, 4)), dma((3, Q)), dma((2,)),
        ],
        compiler_params=pltpu.CompilerParams(
            collective_id=1, has_side_effects=True, vmem_limit_bytes=LIMIT
        ),
    )(y, ym, dx, st_tok, st_cot)


def body(tokens, expert_ids, combine, cotangent, old_layout, pair_moves, gate_w, up_w, down_w):
    at = position()
    xlo, y, z, c = at["xlo"], at["y"], at["z"], at["c"]
    slots = jnp.arange(128, dtype=jnp.int32)
    owner, local = slots // 2, slots % 2
    moved = (local == 1) & (pair_moves[owner] == 1)
    source = jnp.where(moved, (owner + 32) % 64 * 2 + local, slots)
    new_layout = jnp.sum(jnp.where(source[:, None] == slots[None, :], old_layout[None, :], 0), axis=1)
    by_place = new_layout.reshape(2, 4, 4, 4)
    plane = lax.dynamic_index_in_dim(by_place, xlo, 0, False)
    at_y = lax.dynamic_index_in_dim(plane, y, 1, False)
    at_z = lax.dynamic_index_in_dim(plane, z, 0, False)
    own = lax.dynamic_slice(at_z.reshape(16), ((y * 2 + c) * 2,), (2,))
    device = ((xlo * 4 + z) * 4 + y) * 2 + c
    flag = lax.dynamic_slice(pair_moves, (device,), (1,))
    facts = jnp.concatenate([flag, own])
    e_tok = jnp.broadcast_to(at_y.reshape(16, 1), (16, TOK)).astype(F32)
    e_cot = jnp.broadcast_to(at_z.reshape(16, 1), (16, TOK)).astype(F32)

    high = lax.reduce_precision(combine, 8, 7)
    middle = lax.reduce_precision(combine - high, 8, 7)
    low = lax.reduce_precision(combine - high - middle, 8, 7)
    meta = jnp.concatenate(
        [expert_ids.astype(BF), high.astype(BF), middle.astype(BF), low.astype(BF), jnp.zeros((TOK, META - 32), BF)],
        axis=1,
    )
    tok = jnp.concatenate([tokens, meta], axis=1)
    cot = jnp.concatenate([cotangent, meta], axis=1)
    x, dy, st_tok, st_cot, wg_new, wu_new, wd_new = dispatch(tok, cot, e_tok, e_cot, gate_w, up_w, down_w)

    r = jnp.arange(ALL, dtype=jnp.int32)
    there = (r // CAP % 4 * 2 + r // ROWS % 2) * ROWS + (r // (4 * CAP) % 2 * 4 + r // (2 * ROWS)) * CAP + r % CAP
    perm = (there[:, None] == r[None, :]).astype(BF)
    y_rows, y_meta, dx_rows, gg, gu, gd = experts(
        facts, x.reshape(2, ALL, WIDE), dy.reshape(2, ALL, D), perm,
        gate_w, up_w, down_w, wg_new, wu_new, wd_new,
    )
    mixed, d_tokens, d_combine = give_back(
        y_rows.reshape(Q, 2, 8, ROWS, 2 * PART), y_meta.reshape(1, 2, 8, ROWS, META),
        dx_rows.reshape(Q, 2, 8, ROWS, 2 * PART), st_tok, st_cot,
    )
    return mixed, d_tokens, d_combine, gg, gu, gd


def solution(mesh):
    fine = Mesh(mesh.devices.reshape(2, 4, 4, 2, 2), (*EP, "xhi"))
    return jax.shard_map(
        body,
        mesh=fine,
        in_specs=(
            P(EP, None), P(EP, None), P(EP, None), P(EP, None), P(), P(),
            P(EP, None, "xhi"), P(EP, None, "xhi"), P(EP, "xhi", None),
        ),
        out_specs=(
            P(EP, "xhi"), P(EP, "xhi"), P(EP, None),
            P(EP, None, "xhi"), P(EP, None, "xhi"), P(EP, "xhi", None),
        ),
        check_vma=False,
    )
```

```python
import jax
import jax.numpy as jnp
from jax import lax
from jax.experimental import pallas as pl
from jax.experimental.pallas import tpu as pltpu
from jax.sharding import Mesh, PartitionSpec as P

MESH = pl.DeviceIdType.MESH
BF, F32 = jnp.bfloat16, jnp.float32
D, FF, CAP, TOK, TOP = 2048, 384, 12, 128, 8
META = 128
WIDE = META + D
BLOCKS = 8
GROUP, SPAN = 4 * CAP, 4 * TOK
ROWS = BLOCKS * CAP
ALL = BLOCKS * ROWS
HALF = D // 2
Q = 4
PART = HALF // Q
LIMIT = 66 * 1024 * 1024 - 4096
EP = ("xlo", "z", "y", "c")
ANY = pl.BlockSpec(memory_space=pl.ANY)
VMEM = pl.BlockSpec(memory_space=pltpu.VMEM)


def position():
    return {name: lax.axis_index(name) for name in ("xlo", "z", "y", "c", "xhi")}


def greet(devices):
    barrier = pltpu.get_barrier_semaphore()
    for device in devices:
        pl.semaphore_signal(barrier, inc=1, device_id=device, device_id_type=MESH)
    pl.semaphore_wait(barrier, len(devices))


def remote(source, target, send, recv, device):
    return pltpu.make_async_remote_copy(
        src_ref=source,
        dst_ref=target,
        send_sem=send,
        recv_sem=recv,
        device_id=device,
        device_id_type=MESH,
    )


def others(axis, me):
    found = []
    for step in range(1, 8):
        j = lax.rem(me + step, 8)
        found.append({axis: j // 2, "c": lax.rem(j, 2)})
    return found


def expert_at(old_layout, pair_moves, device, l):
    if l == 0:
        return old_layout[device * 2]
    source = jnp.where(pair_moves[device] == 1, lax.rem(device + 32, 64), device)
    return old_layout[source * 2 + 1]


def dispatch_kernel(
    tok_ref, cot_ref, ids_ref, combine_ref, old_layout, pair_moves, wg, wu, wd,
    x_out, dy_out, st_tok_out, st_cot_out, wg_out, wu_out, wd_out, perm_out,
    g0_tok, g1_tok, g0_cot, g1_cot, sel0_tok, sel1_tok, sel0_cot, sel1_cot,
    st_tok, st_cot, code_tok, code_cot, e_tok, e_cot, rowcode, upper, perm,
    ag_send, ag_recv, x_send, x_recv, st_sem, in_sem, loc_sem, w_send, w_recv,
):
    at = position()
    xlo, y, z, c, xhi = at["xlo"], at["y"], at["z"], at["c"], at["xhi"]
    direct, flipped = {"xlo": 1 - xlo}, {"xlo": 1 - xlo, "xhi": 1 - xhi}
    me_z, me_y = z * 2 + c, y * 2 + c

    gathers = (
        (0, tok_ref, (g0_tok, g1_tok), "y", y),
        (1, cot_ref, (g0_cot, g1_cot), "z", z),
    )

    def load(side, h):
        p, source, gathered, axis, a = side
        target = gathered[h].at[xlo * 4 + a]
        if h == 0:
            target = target.at[:, META : META + HALF]
        return pltpu.make_async_copy(source.at[:, h * HALF : (h + 1) * HALF], target, in_sem.at[p, h])

    for h in range(2):
        for side in gathers:
            load(side, h).start()
    w = combine_ref[...]
    high = w.astype(BF).astype(F32)
    middle = (w - high).astype(BF).astype(F32)
    facts = jnp.concatenate(
        [ids_ref[...].astype(F32), high, middle, w - high - middle, jnp.zeros((META - 32, TOK), F32)], axis=0
    )
    meta = facts.T.astype(BF)
    for p, source, gathered, axis, a in gathers:
        gathered[0][xlo * 4 + a, :, 0:META] = meta
    greet([direct, flipped] + others("z", me_z) + others("y", me_y))

    def copies(side, h):
        p, source, gathered, axis, a = side
        held = gathered[h]
        right, left = {axis: lax.rem(a + 1, 4)}, {axis: lax.rem(a + 3, 4)}
        opposite = lax.rem(a + 2, 4)
        mine, theirs = xlo * 4, (1 - xlo) * 4
        l, r = lax.rem(a + 3, 4), lax.rem(a + 1, 4)
        lo, hi = pl.ds(0, 64), pl.ds(64, 64)
        own = held.at[mine + a]
        plan = [
            (own, flipped, held.at[theirs + a]),
            (own, right, held.at[mine + l]),
            (own, left, held.at[mine + r]),
            (held.at[theirs + a], right, held.at[theirs + l]),
            (held.at[theirs + a], left, held.at[theirs + r]),
            (held.at[mine + l, lo], right, held.at[mine + opposite, lo]),
            (held.at[theirs + l, lo], right, held.at[theirs + opposite, lo]),
            (held.at[mine + r, hi], left, held.at[mine + opposite, hi]),
            (held.at[theirs + r, hi], left, held.at[theirs + opposite, hi]),
        ]
        out = [remote(t, t, ag_send.at[p, h, i], ag_recv.at[p, h, i], dev) for i, (t, dev, _) in enumerate(plan)]
        come = [remote(t, got, ag_send.at[p, h, i], ag_recv.at[p, h, i], dev) for i, (t, dev, got) in enumerate(plan)]
        return out, come

    moves = [[copies(side, h) for side in gathers] for h in range(2)]

    def open_half(h):
        for side, (out, _) in zip(gathers, moves[h]):
            load(side, h).wait()
            for i in (1, 2, 0):
                out[i].start()

    def pass_half(h, arrival, starts):
        for out, come in moves[h]:
            come[arrival].wait_recv()
            for i in starts:
                out[i].start()

    def close_half(h):
        for out, come in moves[h]:
            for i in (5, 6, 7, 8):
                come[i].wait_recv()

    open_half(0)
    weights = [
        remote(src.at[1], dst, w_send.at[i], w_recv.at[i], direct)
        for i, (src, dst) in enumerate(((wg, wg_out), (wu, wu_out), (wd, wd_out)))
    ]
    for copy in weights:
        copy.start()

    row = lax.broadcasted_iota(jnp.int32, (GROUP, SPAN), 0)
    col = lax.broadcasted_iota(jnp.int32, (GROUP, SPAN), 1)
    value = jnp.full((GROUP, SPAN), -2, jnp.int32)
    for b in range(4):
        inside = (row >= b * CAP) & (row < (b + 1) * CAP) & (col >= b * TOK) & (col < (b + 1) * TOK)
        value = jnp.where(inside, row - b * CAP, value)
    rowcode[...] = value.astype(F32)
    before = lax.broadcasted_iota(jnp.int32, (TOK, TOK), 0) < lax.broadcasted_iota(jnp.int32, (TOK, TOK), 1)
    upper[...] = jnp.where(before, 1.0, 0.0).astype(BF)
    place = lax.broadcasted_iota(jnp.int32, (16, TOK), 0)
    along_z, along_y = jnp.zeros((16, TOK), jnp.int32), jnp.zeros((16, TOK), jnp.int32)
    for slot in range(16):
        b, core, l = slot // 4, slot // 2 % 2, slot % 2
        found = expert_at(old_layout, pair_moves, ((xlo * 4 + b) * 4 + y) * 2 + core, l)
        along_z = jnp.where(place == slot, found, along_z)
        found = expert_at(old_layout, pair_moves, ((xlo * 4 + z) * 4 + b) * 2 + core, l)
        along_y = jnp.where(place == slot, found, along_y)
    e_tok[...] = along_z.astype(F32)
    e_cot[...] = along_y.astype(F32)

    pass_half(0, 0, (3, 4))
    pass_half(0, 1, (5,))
    pass_half(0, 2, (7,))
    open_half(1)

    def strip(i, carry):
        lr = lax.broadcasted_iota(jnp.int32, (GROUP, ALL), 0)
        lc = lax.broadcasted_iota(jnp.int32, (GROUP, ALL), 1)
        inner = jnp.where(lr >= 12, 1, 0) + jnp.where(lr >= 24, 1, 0) + jnp.where(lr >= 36, 1, 0)
        there = i * GROUP + lr + (2 * ROWS - CAP) * (inner - i // 4)
        perm[pl.ds(pl.multiple_of(i * GROUP, GROUP), GROUP)] = jnp.where(lc == there, 1.0, 0.0).astype(BF)
        return carry

    lax.fori_loop(0, ALL // GROUP, strip, 0)
    perm_copy = pltpu.make_async_copy(perm, perm_out, loc_sem.at[4])
    perm_copy.start()
    pass_half(0, 3, (6,))
    pass_half(0, 4, (8,))
    close_half(0)

    def choose(gathered, experts, code, st):
        for b in range(BLOCKS):
            ids = gathered[b, :, 0:META].astype(F32).T[0:TOP]
            member = jnp.zeros((16, TOK), F32)
            for k in range(TOP):
                member = member + jnp.where(ids[k : k + 1] == experts[...], 1.0, 0.0)
            place = jnp.dot(member.astype(BF), upper[...], preferred_element_type=F32)
            found = jnp.where(member > 0.5, place, -1.0)
            for d in range(8):
                code[d, 0:2, b * TOK : (b + 1) * TOK] = found[2 * d : 2 * d + 2]

        def fill(d, carry):
            rows = code[d]
            for g in range(2):
                for l in range(2):
                    wanted = rows[l : l + 1, g * SPAN : (g + 1) * SPAN]
                    to = pl.ds(pl.multiple_of(d * 2 * GROUP + l * GROUP, GROUP), GROUP)
                    st[g, to] = jnp.where(rowcode[...] == wanted, 1.0, 0.0).astype(BF)
            return carry

        lax.fori_loop(0, 8, fill, 0)

    def emit(pair, gathered, start, sel, st):
        width = sel.shape[-1]
        from_rows = pl.ds(pl.multiple_of(pair * 4 * GROUP, 4 * GROUP), 4 * GROUP)
        for g in range(2):
            source = gathered[g * 4 : (g + 1) * 4, :, start : start + width].reshape(SPAN, width)
            got = jnp.dot(st[g, from_rows], source, preferred_element_type=F32).astype(BF)
            sel[pl.ds(pair * 2, 2), :, g * GROUP : (g + 1) * GROUP] = got.reshape(2, 2, GROUP, width)

    sides = (
        (0, (g0_tok, g1_tok), e_tok, code_tok, (sel0_tok, sel1_tok), st_tok, st_tok_out, x_out, "z", z, (0, META + HALF)),
        (1, (g0_cot, g1_cot), e_cot, code_cot, (sel0_cot, sel1_cot), st_cot, st_cot_out, dy_out, "y", y, (0, HALF)),
    )

    def target(side, h, slot):
        out, sel, start = side[7], side[4][h], side[10][h]
        return out.at[:, slot, :, pl.ds(start, sel.shape[-1])]

    def exchange(side, h, j, slot):
        p, sel, axis = side[0], side[4][h], side[8]
        return remote(
            sel.at[j], target(side, h, slot), x_send.at[p, h, j], x_recv.at[p, h, slot],
            {axis: j // 2, "c": lax.rem(j, 2)},
        )

    def keep(side, h):
        j = side[9] * 2 + c
        return pltpu.make_async_copy(side[4][h].at[j], target(side, h, j), loc_sem.at[2 * side[0] + h])

    def produce(h, i):
        for side in sides:
            p, gathered, experts, code, sel, st, st_out, out, axis, b, starts = side
            pair = lax.rem(b + i, 4)
            skip = META if h == 0 and p == 1 else 0
            emit(pair, gathered[h], skip, sel[h], st)
            if i < 4:
                for core in range(2):
                    exchange(side, h, pair * 2 + core, b * 2 + c).start()
            else:
                exchange(side, h, b * 2 + 1 - c, b * 2 + c).start()
                keep(side, h).start()

    for side in sides:
        p, gathered, experts, code, sel, st, st_out, out, axis, b, starts = side
        choose(gathered[0], experts, code, st)
        pltpu.make_async_copy(st, st_out, st_sem.at[p]).start()
        if p == 0:
            pass_half(1, 0, (3, 4))
    produce(0, 1)
    pass_half(1, 1, (5,))
    pass_half(1, 2, (7,))
    produce(0, 2)
    pass_half(1, 3, (6,))
    pass_half(1, 4, (8,))
    produce(0, 3)
    produce(0, 4)
    close_half(1)
    for i in range(1, 5):
        produce(1, i)

    for h in range(2):

        def finish(i, carry):
            for side in sides:
                j = lax.rem(side[9] * 2 + c + i, 8)
                exchange(side, h, j, j).wait_send()
                exchange(side, h, j, j).wait_recv()
            return carry

        lax.fori_loop(1, 8, finish, 0)
        for side in sides:
            keep(side, h).wait()
        for out, _ in moves[h]:
            for copy in out:
                copy.wait_send()
    for side in sides:
        pltpu.make_async_copy(side[5], side[6], st_sem.at[side[0]]).wait()
    perm_copy.wait()
    for copy in weights:
        copy.wait()


def dispatch(tok, cot, ids, combine, old_layout, pair_moves, wg, wu, wd):
    choice = pltpu.VMEM((2, ALL, SPAN), BF)
    code = pltpu.VMEM((8, 8, BLOCKS * TOK), F32)
    dma = pltpu.SemaphoreType.DMA
    smem = pl.BlockSpec(memory_space=pltpu.SMEM)
    halves = [pltpu.VMEM((BLOCKS, TOK, META + HALF), BF), pltpu.VMEM((BLOCKS, TOK, HALF), BF)]
    wide, narrow = pltpu.VMEM((8, 2, ROWS, META + HALF), BF), pltpu.VMEM((8, 2, ROWS, HALF), BF)
    return pl.pallas_call(
        dispatch_kernel,
        name="dispatch",
        out_shape=(
            jax.ShapeDtypeStruct((2, 8, ROWS, WIDE), BF),
            jax.ShapeDtypeStruct((2, 8, ROWS, D), BF),
            jax.ShapeDtypeStruct((2, ALL, SPAN), BF),
            jax.ShapeDtypeStruct((2, ALL, SPAN), BF),
            jax.ShapeDtypeStruct((D, FF), BF),
            jax.ShapeDtypeStruct((D, FF), BF),
            jax.ShapeDtypeStruct((FF, D), BF),
            jax.ShapeDtypeStruct((ALL, ALL), BF),
        ),
        in_specs=[ANY, ANY, VMEM, VMEM, smem, smem, ANY, ANY, ANY],
        out_specs=[ANY] * 8,
        scratch_shapes=[
            *halves, *halves, wide, narrow, narrow, narrow,
            choice, choice, code, code, pltpu.VMEM((16, TOK), F32), pltpu.VMEM((16, TOK), F32),
            pltpu.VMEM((GROUP, SPAN), F32), pltpu.VMEM((TOK, TOK), BF), pltpu.VMEM((ALL, ALL), BF),
            dma((2, 2, 9)), dma((2, 2, 9)), dma((2, 2, 8)), dma((2, 2, 8)), dma((2,)), dma((2, 2)), dma((5,)),
            dma((3,)), dma((3,)),
        ],
        compiler_params=pltpu.CompilerParams(
            collective_id=0, has_side_effects=True, vmem_limit_bytes=LIMIT
        ),
    )(tok, cot, ids, combine, old_layout, pair_moves, wg, wu, wd)


def expert_kernel(
    old_layout, pair_moves, x, dy, perm, wg, wu, wd, wg_new, wu_new, wd_new,
    y, ym, dx, gg, gu, gd,
    vg, vu, vd, gate, upper, dh_hi, dh_lo, hid, dgate, dup, hid_c, dgate_c, dup_c, sem,
):
    l = pl.program_id(0)
    at = position()
    device = ((at["xlo"] * 4 + at["z"]) * 4 + at["y"]) * 2 + at["c"]
    moved = pair_moves[device] == 1
    pairs = ((wg, wg_new, vg), (wu, wu_new, vu), (wd, wd_new, vd))

    @pl.when(l == 0)
    def _():
        for i, (old, new, held) in enumerate(pairs):
            pltpu.make_async_copy(old.at[0], held.at[0], sem.at[0, i]).start()
        for i, (old, new, held) in enumerate(pairs):

            @pl.when(moved)
            def _(new=new, held=held, i=i):
                pltpu.make_async_copy(new, held.at[1], sem.at[1, i]).start()

            @pl.when(jnp.logical_not(moved))
            def _(old=old, held=held, i=i):
                pltpu.make_async_copy(old.at[1], held.at[1], sem.at[1, i]).start()

    for i, (old, new, held) in enumerate(pairs):
        pltpu.make_async_copy(old.at[0], held.at[l], sem.at[l, i]).wait()
    expert = jnp.where(
        l == 0, expert_at(old_layout, pair_moves, device, 0), expert_at(old_layout, pair_moves, device, 1)
    ).astype(F32)

    def nt(a, b):
        return lax.dot_general(a, b, (((1,), (1,)), ((), ())), preferred_element_type=F32)

    def tn(a, b):
        return lax.dot_general(a, b, (((0,), (0,)), ((), ())), preferred_element_type=F32)

    def nn(a, b):
        return jnp.dot(a, b, preferred_element_type=F32)

    def first(i, carry):
        rows = pl.ds(pl.multiple_of(i * 384, 384), 384)
        own = x[0, rows, META:WIDE]
        gate[rows] = nn(own, vg[l])
        upper[rows] = nn(own, vu[l])
        dh = nt(dy[0, rows], vd[l])
        high = dh.astype(BF)
        dh_hi[rows] = high
        dh_lo[rows] = (dh - high.astype(F32)).astype(BF)
        return carry

    lax.fori_loop(0, ALL // 384, first, 0)

    def second(i, carry):
        rows = pl.ds(pl.multiple_of(i * 192, 192), 192)
        order = perm[rows]
        dh = nn(order, dh_hi[...]) + nn(order, dh_lo[...])
        g, u = gate[rows], upper[rows]
        sigma = jax.nn.sigmoid(g)
        active = g * sigma
        hidden = active * u
        meta = x[0, rows, 0:META].astype(F32)
        lane = lax.broadcasted_iota(jnp.int32, meta.shape, 1)
        named = jnp.where((meta == expert) & (lane < TOP), 1.0, 0.0)
        weight = pltpu.roll(meta, META - 8, 1) + (
            pltpu.roll(meta, META - 16, 1) + pltpu.roll(meta, META - 24, 1)
        )
        w = jnp.sum(named * weight, axis=1, keepdims=True)
        dc = jnp.sum(hidden * dh, axis=1, keepdims=True)
        ym[0, rows] = (named * dc).astype(BF)
        hid[rows] = (hidden * w).astype(BF)
        dh = dh * w
        dgate[rows] = (dh * u * sigma * (1.0 + g * (1.0 - sigma))).astype(BF)
        dup[rows] = (dh * active).astype(BF)
        return carry

    lax.fori_loop(0, ALL // 192, second, 0)

    def store(ref, rows, value):
        for q in range(Q):
            for t in range(2):
                start = t * HALF + q * PART
                ref[q, 0, rows, t * PART : (t + 1) * PART] = value[:, start : start + PART]

    def third(i, carry):
        rows = pl.ds(pl.multiple_of(i * 192, 192), 192)
        order = perm[rows]
        store(y, rows, nn(hid[rows], vd[l]).astype(BF))
        a = nn(order, dgate[...]).astype(BF)
        b = nn(order, dup[...]).astype(BF)
        hid_c[rows] = nn(order, hid[...]).astype(BF)
        store(dx, rows, (nt(a, vg[l]) + nt(b, vu[l])).astype(BF))
        return carry

    lax.fori_loop(0, ALL // 192, third, 0)

    def fourth(i, carry):
        cols = pl.ds(pl.multiple_of(i * 512, 512), 512)
        own = x[0, :, pl.ds(pl.multiple_of(META + i * 512, 128), 512)]
        gg[0, cols] = tn(own, dgate[...]).astype(BF)
        gu[0, cols] = tn(own, dup[...]).astype(BF)
        gd[0, :, cols] = tn(hid_c[...], dy[0, :, cols]).astype(BF)
        return carry

    lax.fori_loop(0, D // 512, fourth, 0)


def experts(old_layout, pair_moves, x, dy, perm, wg, wu, wd, wg_new, wu_new, wd_new):
    def block(*shape):
        return pl.BlockSpec((1, *shape), lambda l: (l,) + (0,) * len(shape))

    parts = pl.BlockSpec((Q, 1, ALL, 2 * PART), lambda l: (0, l, 0, 0))
    small = pltpu.VMEM((ALL, FF), BF)
    wide = pltpu.VMEM((ALL, FF), F32)
    return pl.pallas_call(
        expert_kernel,
        name="experts",
        grid=(2,),
        out_shape=(
            jax.ShapeDtypeStruct((Q, 2, ALL, 2 * PART), BF),
            jax.ShapeDtypeStruct((2, ALL, META), BF),
            jax.ShapeDtypeStruct((Q, 2, ALL, 2 * PART), BF),
            jax.ShapeDtypeStruct((2, D, FF), BF),
            jax.ShapeDtypeStruct((2, D, FF), BF),
            jax.ShapeDtypeStruct((2, FF, D), BF),
        ),
        in_specs=[
            pl.BlockSpec(memory_space=pltpu.SMEM), pl.BlockSpec(memory_space=pltpu.SMEM),
            block(ALL, WIDE), block(ALL, D),
            pl.BlockSpec((ALL, ALL), lambda l: (0, 0), pipeline_mode=pl.Buffered(1)),
            ANY, ANY, ANY, ANY, ANY, ANY,
        ],
        out_specs=[parts, block(ALL, META), parts, block(D, FF), block(D, FF), block(FF, D)],
        scratch_shapes=[
            pltpu.VMEM((2, D, FF), BF), pltpu.VMEM((2, D, FF), BF), pltpu.VMEM((2, FF, D), BF),
            wide, wide, small, small, small, small, small, small, small, small,
            pltpu.SemaphoreType.DMA((2, 3)),
        ],
        compiler_params=pltpu.CompilerParams(
            dimension_semantics=("arbitrary",), vmem_limit_bytes=LIMIT
        ),
    )(old_layout, pair_moves, x, dy, perm, wg, wu, wd, wg_new, wu_new, wd_new)


def return_kernel(
    y_ref, ym_ref, dx_ref, st_tok, st_cot,
    mixed, d_tokens, d_combine,
    c_tok, c_meta, c_cot, raw_tok, raw_cot, s_tok, s_cot, m_tok, m_meta, m_cot,
    h_tok, h_meta, h_cot, rx_tok, rx_meta, rx_cot, xs_tok, xs_meta, xs_cot, ra_tok, ra_meta, ra_cot,
    a_send, a_recv, h_send, h_recv, x_send, x_recv, f_send, f_recv, loc_sem, st_sem,
):
    at = position()
    xlo, y, z, c, xhi = at["xlo"], at["y"], at["z"], at["c"], at["xhi"]
    near = ({"xlo": 1 - xlo}, {"xlo": 1 - xlo, "xhi": 1 - xhi})
    their_t = (xhi, 1 - xhi)
    greet([*near, *others("z", z * 2 + c), *others("y", y * 2 + c)])

    tok = (0, y_ref, c_tok, s_tok, m_tok, h_tok, rx_tok, xs_tok, ra_tok, "z", z * 2 + c, "y", y)
    cot = (1, dx_ref, c_cot, s_cot, m_cot, h_cot, rx_cot, xs_cot, ra_cot, "y", y * 2 + c, "z", z)
    small = (2, ym_ref, c_meta, s_tok, m_meta, h_meta, rx_meta, xs_meta, ra_meta, "z", z * 2 + c, "y", y)

    def exchange(side, q, j, slot):
        p, source, held, s, m, h, rx, xs, ra, axis, me, other, a = side
        return remote(
            source.at[q, :, j], held.at[q, slot], a_send.at[p, q, j], a_recv.at[p, q, slot],
            {axis: j // 2, "c": lax.rem(j, 2)},
        )

    def own(side, q):
        p, source, held, s, m, h, rx, xs, ra, axis, me, other, a = side
        return pltpu.make_async_copy(source.at[q, :, me], held.at[q, me], loc_sem.at[p, q])

    def relay(side, q, k):
        p, source, held, s, m, h, rx, xs, ra, axis, me, other, a = side
        piece = m.at[q, xlo, 0 if p == 2 else 1 - xhi, pl.ds(2 * k, 2)]
        return remote(piece, h.at[q, k], h_send.at[p, q, k], h_recv.at[p, q, k], near[k])

    def spread(side, q, k):
        p, source, held, s, m, h, rx, xs, ra, axis, me, other, a = side
        piece = m.at[q, 1 - xlo, k if p == 2 else their_t[k]]
        return remote(piece, rx.at[q, k], x_send.at[p, q, k], x_recv.at[p, q, k], near[k])

    def fold(side, q, k, slot):
        p, source, held, s, m, h, rx, xs, ra, axis, me, other, a = side
        to = lax.rem(a + k, 4)
        return remote(xs.at[q, to], ra.at[q, slot], f_send.at[p, q, k], f_recv.at[p, q, k], {other: to})

    def begin(side, q):
        def send(i, carry):
            exchange(side, q, lax.rem(side[10] + i, 8), side[10]).start()
            return carry

        lax.fori_loop(1, 8, send, 0)
        own(side, q).start()

    def begin_part(q, carry):
        begin(tok, q)
        begin(cot, q)
        return carry

    begin(small, 0)
    lax.fori_loop(0, Q, begin_part, 0)
    loads = [
        pltpu.make_async_copy(src, raw, st_sem.at[i]) for i, (src, raw) in enumerate(((st_tok, raw_tok), (st_cot, raw_cot)))
    ]
    for load in loads:
        load.start()
    for load, raw, s in ((loads[0], raw_tok, s_tok), (loads[1], raw_cot, s_cot)):
        load.wait()
        for g in range(2):

            def turn(n, carry, raw=raw, s=s, g=g):
                cols = pl.ds(pl.multiple_of(n * 128, 128), 128)
                s[g, cols] = raw[g, :, cols].astype(F32).T.astype(BF)
                return carry

            lax.fori_loop(0, SPAN // 128, turn, 0)

    def combine(side, q):
        p, source, held, s, m, h, rx, xs, ra, axis, me, other, a = side

        def arrive(i, carry):
            j = lax.rem(me + i, 8)
            exchange(side, q, j, j).wait_recv()
            return carry

        lax.fori_loop(1, 8, arrive, 0)
        own(side, q).wait()
        size = held.shape[-1]
        for g in range(2):
            part = held[q, :, :, g * GROUP : (g + 1) * GROUP].reshape(ALL, size)
            got = jnp.dot(s[g], part, preferred_element_type=F32).astype(BF)
            if p == 2:
                for t in range(2):
                    m[q, g, t] = got.reshape(4, TOK, META)
            else:
                for t in range(2):
                    m[q, g, t] = got[:, t * PART : (t + 1) * PART].reshape(4, TOK, PART)
        for k in range(2):
            relay(side, q, k).start()

    def pass_on(side, q):
        p, source, held, s, m, h, rx, xs, ra, axis, me, other, a = side
        for k in range(2):
            relay(side, q, k).wait_recv()
            t = (1 - k) if p == 2 else their_t[1 - k]
            half = pl.ds(2 * k, 2)
            total = m[q, 1 - xlo, t, half].astype(F32) + h[q, k].astype(F32)
            m[q, 1 - xlo, t, half] = total.astype(BF)
        for k in range(2):
            spread(side, q, k).start()

    def gather(side, q):
        p, source, held, s, m, h, rx, xs, ra, axis, me, other, a = side
        for k in range(2):
            spread(side, q, k).wait_recv()
        total = m[q, xlo, 0 if p == 2 else xhi].astype(F32)
        for k in range(2):
            total = total + rx[q, k].astype(F32)
        xs[q] = total.astype(BF)
        for k in range(1, 4):
            fold(side, q, k, a).start()

    def close(side, q):
        p, source, held, s, m, h, rx, xs, ra, axis, me, other, a = side
        for k in range(1, 4):
            fold(side, q, k, a).wait_recv()
        total = xs[q, a].astype(F32)
        for k in range(1, 4):
            total = total + ra[q, lax.rem(a + k, 4)].astype(F32)
        if p == 2:
            d_combine[...] = total.T[0:TOP]
        else:
            (mixed, d_tokens)[p][:, pl.ds(pl.multiple_of(q * PART, PART), PART)] = total.astype(BF)
        for k in range(2):
            relay(side, q, k).wait_send()
            spread(side, q, k).wait_send()
            fold(side, q, k + 1, a).wait_send()
        fold(side, q, 3, a).wait_send()

        def sent(i, carry):
            exchange(side, q, lax.rem(me + i, 8), me).wait_send()
            return carry

        lax.fori_loop(1, 8, sent, 0)

    def both(stage, q):
        stage(tok, q)
        stage(cot, q)

    combine(small, 0)
    both(combine, 0)
    pass_on(small, 0)
    both(pass_on, 0)
    both(combine, 1)
    gather(small, 0)
    both(gather, 0)
    both(pass_on, 1)

    def flow(q, carry):
        both(combine, q)
        both(gather, q - 1)
        both(pass_on, q)
        both(close, q - 2)
        return carry

    lax.fori_loop(2, Q, flow, 0)
    close(small, 0)
    both(gather, Q - 1)
    both(close, Q - 2)
    both(close, Q - 1)


def give_back(y, ym, dx, st_tok, st_cot):
    dma = pltpu.SemaphoreType.DMA

    def each(*shape):
        return [
            pltpu.VMEM((Q, *shape, PART), BF), pltpu.VMEM((1, *shape, META), BF), pltpu.VMEM((Q, *shape, PART), BF)
        ]

    held = (8, 2, ROWS)
    return pl.pallas_call(
        return_kernel,
        name="give_back",
        out_shape=(
            jax.ShapeDtypeStruct((TOK, HALF), BF),
            jax.ShapeDtypeStruct((TOK, HALF), BF),
            jax.ShapeDtypeStruct((TOP, TOK), F32),
        ),
        in_specs=[ANY] * 5,
        out_specs=[VMEM] * 3,
        scratch_shapes=[
            pltpu.VMEM((Q, *held, 2 * PART), BF), pltpu.VMEM((1, *held, META), BF), pltpu.VMEM((Q, *held, 2 * PART), BF),
            pltpu.VMEM((2, ALL, SPAN), BF), pltpu.VMEM((2, ALL, SPAN), BF),
            pltpu.VMEM((2, SPAN, ALL), BF), pltpu.VMEM((2, SPAN, ALL), BF),
            *each(2, 2, 4, TOK), *each(2, 2, TOK), *each(2, 4, TOK), *each(4, TOK), *each(4, TOK),
            dma((3, Q, 8)), dma((3, Q, 8)), dma((3, Q, 2)), dma((3, Q, 2)), dma((3, Q, 2)), dma((3, Q, 2)),
            dma((3, Q, 4)), dma((3, Q, 4)), dma((3, Q)), dma((2,)),
        ],
        compiler_params=pltpu.CompilerParams(
            collective_id=1, has_side_effects=True, vmem_limit_bytes=LIMIT
        ),
    )(y, ym, dx, st_tok, st_cot)


def body(tokens, expert_ids, combine, cotangent, old_layout, pair_moves, gate_w, up_w, down_w):
    x, dy, st_tok, st_cot, wg_new, wu_new, wd_new, perm = dispatch(
        tokens, cotangent, expert_ids.T, combine.T, old_layout, pair_moves, gate_w, up_w, down_w
    )
    y_rows, y_meta, dx_rows, gg, gu, gd = experts(
        old_layout, pair_moves, x.reshape(2, ALL, WIDE), dy.reshape(2, ALL, D), perm,
        gate_w, up_w, down_w, wg_new, wu_new, wd_new,
    )
    mixed, d_tokens, d_combine = give_back(
        y_rows.reshape(Q, 2, 8, ROWS, 2 * PART), y_meta.reshape(1, 2, 8, ROWS, META),
        dx_rows.reshape(Q, 2, 8, ROWS, 2 * PART), st_tok, st_cot,
    )
    return mixed, d_tokens, d_combine.T, gg, gu, gd


def solution(mesh):
    fine = Mesh(mesh.devices.reshape(2, 4, 4, 2, 2), (*EP, "xhi"))
    return jax.shard_map(
        body,
        mesh=fine,
        in_specs=(
            P(EP, None), P(EP, None), P(EP, None), P(EP, None), P(), P(),
            P(EP, None, "xhi"), P(EP, None, "xhi"), P(EP, "xhi", None),
        ),
        out_specs=(
            P(EP, "xhi"), P(EP, "xhi"), P(EP, None),
            P(EP, None, "xhi"), P(EP, None, "xhi"), P(EP, "xhi", None),
        ),
        check_vma=False,
    )
```

```python
import jax
import jax.numpy as jnp
from jax import lax
from jax.experimental import pallas as pl
from jax.experimental.pallas import tpu as pltpu
from jax.sharding import Mesh, PartitionSpec as P

MESH = pl.DeviceIdType.MESH
BF, F32 = jnp.bfloat16, jnp.float32
D, FF, CAP, TOK, TOP = 2048, 384, 12, 128, 8
META = 128
WIDE = META + D
BLOCKS = 8
GROUP, SPAN = 4 * CAP, 4 * TOK
ROWS = BLOCKS * CAP
ALL = BLOCKS * ROWS
HALF = D // 2
Q = 4
PART = HALF // Q
LIMIT = 66 * 1024 * 1024 - 4096
EP = ("xlo", "z", "y", "c")
ANY = pl.BlockSpec(memory_space=pl.ANY)
VMEM = pl.BlockSpec(memory_space=pltpu.VMEM)


def position():
    return {name: lax.axis_index(name) for name in ("xlo", "z", "y", "c", "xhi")}


def greet(devices):
    barrier = pltpu.get_barrier_semaphore()
    for device in devices:
        pl.semaphore_signal(barrier, inc=1, device_id=device, device_id_type=MESH)
    pl.semaphore_wait(barrier, len(devices))


def remote(source, target, send, recv, device):
    return pltpu.make_async_remote_copy(
        src_ref=source,
        dst_ref=target,
        send_sem=send,
        recv_sem=recv,
        device_id=device,
        device_id_type=MESH,
    )


def others(axis, me):
    found = []
    for step in range(1, 8):
        j = lax.rem(me + step, 8)
        found.append({axis: j // 2, "c": lax.rem(j, 2)})
    return found


def expert_at(old_layout, pair_moves, device, l):
    if l == 0:
        return old_layout[device * 2]
    source = jnp.where(pair_moves[device] == 1, lax.rem(device + 32, 64), device)
    return old_layout[source * 2 + 1]


def dispatch_kernel(
    tok_ref, cot_ref, ids_ref, combine_ref, old_layout, pair_moves, wg, wu, wd,
    x_out, dy_out, st_tok_out, st_cot_out, wg_out, wu_out, wd_out, perm_out,
    g0_tok, g1_tok, g0_cot, g1_cot, sel0_tok, sel1_tok, sel0_cot, sel1_cot,
    st_tok, st_cot, code_tok, code_cot, e_tok, e_cot, rowcode, upper, perm,
    ag_send, ag_recv, x_send, x_recv, st_sem, in_sem, loc_sem, w_send, w_recv,
):
    at = position()
    xlo, y, z, c, xhi = at["xlo"], at["y"], at["z"], at["c"], at["xhi"]
    direct, flipped = {"xlo": 1 - xlo}, {"xlo": 1 - xlo, "xhi": 1 - xhi}
    me_z, me_y = z * 2 + c, y * 2 + c

    gathers = (
        (0, tok_ref, (g0_tok, g1_tok), "y", y),
        (1, cot_ref, (g0_cot, g1_cot), "z", z),
    )

    def load(side, h):
        p, source, gathered, axis, a = side
        target = gathered[h].at[xlo * 4 + a]
        if h == 0:
            target = target.at[:, META : META + HALF]
        return pltpu.make_async_copy(source.at[:, h * HALF : (h + 1) * HALF], target, in_sem.at[p, h])

    for h in range(2):
        for side in gathers:
            load(side, h).start()
    w = combine_ref[...]
    high = w.astype(BF).astype(F32)
    middle = (w - high).astype(BF).astype(F32)
    facts = jnp.concatenate(
        [ids_ref[...].astype(F32), high, middle, w - high - middle, jnp.zeros((META - 32, TOK), F32)], axis=0
    )
    meta = facts.T.astype(BF)
    for p, source, gathered, axis, a in gathers:
        gathered[0][xlo * 4 + a, :, 0:META] = meta
    greet([direct, flipped] + others("z", me_z) + others("y", me_y))

    def copies(side, h):
        p, source, gathered, axis, a = side
        held = gathered[h]
        right, left = {axis: lax.rem(a + 1, 4)}, {axis: lax.rem(a + 3, 4)}
        opposite = lax.rem(a + 2, 4)
        mine, theirs = xlo * 4, (1 - xlo) * 4
        l, r = lax.rem(a + 3, 4), lax.rem(a + 1, 4)
        lo, hi = pl.ds(0, 64), pl.ds(64, 64)
        own = held.at[mine + a]
        plan = [
            (own, flipped, held.at[theirs + a]),
            (own, right, held.at[mine + l]),
            (own, left, held.at[mine + r]),
            (held.at[theirs + a], right, held.at[theirs + l]),
            (held.at[theirs + a], left, held.at[theirs + r]),
            (held.at[mine + l, lo], right, held.at[mine + opposite, lo]),
            (held.at[theirs + l, lo], right, held.at[theirs + opposite, lo]),
            (held.at[mine + r, hi], left, held.at[mine + opposite, hi]),
            (held.at[theirs + r, hi], left, held.at[theirs + opposite, hi]),
        ]
        out = [remote(t, t, ag_send.at[p, h, i], ag_recv.at[p, h, i], dev) for i, (t, dev, _) in enumerate(plan)]
        come = [remote(t, got, ag_send.at[p, h, i], ag_recv.at[p, h, i], dev) for i, (t, dev, got) in enumerate(plan)]
        return out, come

    moves = [[copies(side, h) for side in gathers] for h in range(2)]

    def open_half(h):
        for side, (out, _) in zip(gathers, moves[h]):
            load(side, h).wait()
            for i in (1, 2, 0):
                out[i].start()

    def pass_half(h, arrival, starts):
        for out, come in moves[h]:
            come[arrival].wait_recv()
            for i in starts:
                out[i].start()

    def close_half(h):
        for out, come in moves[h]:
            for i in (5, 6, 7, 8):
                come[i].wait_recv()

    open_half(0)
    weights = [
        remote(src.at[1], dst, w_send.at[i], w_recv.at[i], direct)
        for i, (src, dst) in enumerate(((wg, wg_out), (wu, wu_out), (wd, wd_out)))
    ]
    for copy in weights:
        copy.start()

    row = lax.broadcasted_iota(jnp.int32, (GROUP, SPAN), 0)
    col = lax.broadcasted_iota(jnp.int32, (GROUP, SPAN), 1)
    value = jnp.full((GROUP, SPAN), -2, jnp.int32)
    for b in range(4):
        inside = (row >= b * CAP) & (row < (b + 1) * CAP) & (col >= b * TOK) & (col < (b + 1) * TOK)
        value = jnp.where(inside, row - b * CAP, value)
    rowcode[...] = value.astype(F32)
    before = lax.broadcasted_iota(jnp.int32, (TOK, TOK), 0) < lax.broadcasted_iota(jnp.int32, (TOK, TOK), 1)
    upper[...] = jnp.where(before, 1.0, 0.0).astype(BF)
    place = lax.broadcasted_iota(jnp.int32, (16, TOK), 0)
    along_z, along_y = jnp.zeros((16, TOK), jnp.int32), jnp.zeros((16, TOK), jnp.int32)
    for slot in range(16):
        b, core, l = slot // 4, slot // 2 % 2, slot % 2
        found = expert_at(old_layout, pair_moves, ((xlo * 4 + b) * 4 + y) * 2 + core, l)
        along_z = jnp.where(place == slot, found, along_z)
        found = expert_at(old_layout, pair_moves, ((xlo * 4 + z) * 4 + b) * 2 + core, l)
        along_y = jnp.where(place == slot, found, along_y)
    e_tok[...] = along_z.astype(F32)
    e_cot[...] = along_y.astype(F32)

    pass_half(0, 0, (3, 4))
    pass_half(0, 1, (5,))
    pass_half(0, 2, (7,))
    open_half(1)

    def strip(i, carry):
        lr = lax.broadcasted_iota(jnp.int32, (GROUP, ALL), 0)
        lc = lax.broadcasted_iota(jnp.int32, (GROUP, ALL), 1)
        inner = jnp.where(lr >= 12, 1, 0) + jnp.where(lr >= 24, 1, 0) + jnp.where(lr >= 36, 1, 0)
        there = i * GROUP + lr + (2 * ROWS - CAP) * (inner - i // 4)
        perm[pl.ds(pl.multiple_of(i * GROUP, GROUP), GROUP)] = jnp.where(lc == there, 1.0, 0.0).astype(BF)
        return carry

    lax.fori_loop(0, ALL // GROUP, strip, 0)
    perm_copy = pltpu.make_async_copy(perm, perm_out, loc_sem.at[4])
    perm_copy.start()
    pass_half(0, 3, (6,))
    pass_half(0, 4, (8,))
    close_half(0)

    def choose(gathered, experts, code, st):
        for b in range(BLOCKS):
            ids = gathered[b, :, 0:META].astype(F32).T[0:TOP]
            member = jnp.zeros((16, TOK), F32)
            for k in range(TOP):
                member = member + jnp.where(ids[k : k + 1] == experts[...], 1.0, 0.0)
            place = jnp.dot(member.astype(BF), upper[...], preferred_element_type=F32)
            found = jnp.where(member > 0.5, place, -1.0)
            for d in range(8):
                code[d, 0:2, b * TOK : (b + 1) * TOK] = found[2 * d : 2 * d + 2]

        def fill(d, carry):
            rows = code[d]
            for g in range(2):
                for l in range(2):
                    wanted = rows[l : l + 1, g * SPAN : (g + 1) * SPAN]
                    to = pl.ds(pl.multiple_of(d * 2 * GROUP + l * GROUP, GROUP), GROUP)
                    st[g, to] = jnp.where(rowcode[...] == wanted, 1.0, 0.0).astype(BF)
            return carry

        lax.fori_loop(0, 8, fill, 0)

    def emit(pair, gathered, start, sel, st):
        width = sel.shape[-1]
        from_rows = pl.ds(pl.multiple_of(pair * 4 * GROUP, 4 * GROUP), 4 * GROUP)
        for g in range(2):
            source = gathered[g * 4 : (g + 1) * 4, :, start : start + width].reshape(SPAN, width)
            got = jnp.dot(st[g, from_rows], source, preferred_element_type=F32).astype(BF)
            sel[pl.ds(pair * 2, 2), :, g * GROUP : (g + 1) * GROUP] = got.reshape(2, 2, GROUP, width)

    sides = (
        (0, (g0_tok, g1_tok), e_tok, code_tok, (sel0_tok, sel1_tok), st_tok, st_tok_out, x_out, "z", z, (0, META + HALF)),
        (1, (g0_cot, g1_cot), e_cot, code_cot, (sel0_cot, sel1_cot), st_cot, st_cot_out, dy_out, "y", y, (0, HALF)),
    )

    def target(side, h, slot):
        out, sel, start = side[7], side[4][h], side[10][h]
        return out.at[:, slot, :, pl.ds(start, sel.shape[-1])]

    def exchange(side, h, j, slot):
        p, sel, axis = side[0], side[4][h], side[8]
        return remote(
            sel.at[j], target(side, h, slot), x_send.at[p, h, j], x_recv.at[p, h, slot],
            {axis: j // 2, "c": lax.rem(j, 2)},
        )

    def keep(side, h):
        j = side[9] * 2 + c
        return pltpu.make_async_copy(side[4][h].at[j], target(side, h, j), loc_sem.at[2 * side[0] + h])

    def produce(h, i):
        for side in sides:
            p, gathered, experts, code, sel, st, st_out, out, axis, b, starts = side
            pair = lax.rem(b + i, 4)
            skip = META if h == 0 and p == 1 else 0
            emit(pair, gathered[h], skip, sel[h], st)
            if i < 4:
                for core in range(2):
                    exchange(side, h, pair * 2 + core, b * 2 + c).start()
            else:
                exchange(side, h, b * 2 + 1 - c, b * 2 + c).start()
                keep(side, h).start()

    for side in sides:
        p, gathered, experts, code, sel, st, st_out, out, axis, b, starts = side
        choose(gathered[0], experts, code, st)
        pltpu.make_async_copy(st, st_out, st_sem.at[p]).start()
        if p == 0:
            pass_half(1, 0, (3, 4))
    produce(0, 1)
    pass_half(1, 1, (5,))
    pass_half(1, 2, (7,))
    produce(0, 2)
    pass_half(1, 3, (6,))
    pass_half(1, 4, (8,))
    produce(0, 3)
    produce(0, 4)
    close_half(1)
    for i in range(1, 5):
        produce(1, i)

    for h in range(2):

        def finish(i, carry):
            for side in sides:
                j = lax.rem(side[9] * 2 + c + i, 8)
                exchange(side, h, j, j).wait_send()
                exchange(side, h, j, j).wait_recv()
            return carry

        lax.fori_loop(1, 8, finish, 0)
        for side in sides:
            keep(side, h).wait()
        for out, _ in moves[h]:
            for copy in out:
                copy.wait_send()
    for side in sides:
        pltpu.make_async_copy(side[5], side[6], st_sem.at[side[0]]).wait()
    perm_copy.wait()
    for copy in weights:
        copy.wait()


def dispatch(tok, cot, ids, combine, old_layout, pair_moves, wg, wu, wd):
    choice = pltpu.VMEM((2, ALL, SPAN), BF)
    code = pltpu.VMEM((8, 8, BLOCKS * TOK), F32)
    dma = pltpu.SemaphoreType.DMA
    smem = pl.BlockSpec(memory_space=pltpu.SMEM)
    halves = [pltpu.VMEM((BLOCKS, TOK, META + HALF), BF), pltpu.VMEM((BLOCKS, TOK, HALF), BF)]
    wide, narrow = pltpu.VMEM((8, 2, ROWS, META + HALF), BF), pltpu.VMEM((8, 2, ROWS, HALF), BF)
    return pl.pallas_call(
        dispatch_kernel,
        name="dispatch",
        out_shape=(
            jax.ShapeDtypeStruct((2, 8, ROWS, WIDE), BF),
            jax.ShapeDtypeStruct((2, 8, ROWS, D), BF),
            jax.ShapeDtypeStruct((2, ALL, SPAN), BF),
            jax.ShapeDtypeStruct((2, ALL, SPAN), BF),
            jax.ShapeDtypeStruct((D, FF), BF),
            jax.ShapeDtypeStruct((D, FF), BF),
            jax.ShapeDtypeStruct((FF, D), BF),
            jax.ShapeDtypeStruct((ALL, ALL), BF),
        ),
        in_specs=[ANY, ANY, VMEM, VMEM, smem, smem, ANY, ANY, ANY],
        out_specs=[ANY] * 8,
        scratch_shapes=[
            *halves, *halves, wide, narrow, narrow, narrow,
            choice, choice, code, code, pltpu.VMEM((16, TOK), F32), pltpu.VMEM((16, TOK), F32),
            pltpu.VMEM((GROUP, SPAN), F32), pltpu.VMEM((TOK, TOK), BF), pltpu.VMEM((ALL, ALL), BF),
            dma((2, 2, 9)), dma((2, 2, 9)), dma((2, 2, 8)), dma((2, 2, 8)), dma((2,)), dma((2, 2)), dma((5,)),
            dma((3,)), dma((3,)),
        ],
        compiler_params=pltpu.CompilerParams(
            collective_id=0, has_side_effects=True, vmem_limit_bytes=LIMIT
        ),
    )(tok, cot, ids, combine, old_layout, pair_moves, wg, wu, wd)


def expert_kernel(
    old_layout, pair_moves, x, dy, perm, wg, wu, wd, wg_new, wu_new, wd_new,
    y, ym, dx, gg, gu, gd,
    y_v, dx_v, vg, vu, vd, gate, upper, dh_hi, dh_lo, hid, dgate, dup, hid_c, dgate_c, dup_c, sem, out_sem,
):
    l = pl.program_id(0)
    at = position()
    device = ((at["xlo"] * 4 + at["z"]) * 4 + at["y"]) * 2 + at["c"]
    moved = pair_moves[device] == 1
    pairs = ((wg, wg_new, vg), (wu, wu_new, vu), (wd, wd_new, vd))

    @pl.when(l == 0)
    def _():
        for i, (old, new, held) in enumerate(pairs):
            pltpu.make_async_copy(old.at[0], held.at[0], sem.at[0, i]).start()
        for i, (old, new, held) in enumerate(pairs):

            @pl.when(moved)
            def _(new=new, held=held, i=i):
                pltpu.make_async_copy(new, held.at[1], sem.at[1, i]).start()

            @pl.when(jnp.logical_not(moved))
            def _(old=old, held=held, i=i):
                pltpu.make_async_copy(old.at[1], held.at[1], sem.at[1, i]).start()

    for i, (old, new, held) in enumerate(pairs):
        pltpu.make_async_copy(old.at[0], held.at[l], sem.at[l, i]).wait()
    expert = jnp.where(
        l == 0, expert_at(old_layout, pair_moves, device, 0), expert_at(old_layout, pair_moves, device, 1)
    ).astype(F32)

    def nt(a, b):
        return lax.dot_general(a, b, (((1,), (1,)), ((), ())), preferred_element_type=F32)

    def tn(a, b):
        return lax.dot_general(a, b, (((0,), (0,)), ((), ())), preferred_element_type=F32)

    def nn(a, b):
        return jnp.dot(a, b, preferred_element_type=F32)

    def first(i, carry):
        rows = pl.ds(pl.multiple_of(i * 384, 384), 384)
        own = x[0, rows, META:WIDE]
        gate[rows] = nn(own, vg[l])
        upper[rows] = nn(own, vu[l])
        dh = nt(dy[0, rows], vd[l])
        high = dh.astype(BF)
        dh_hi[rows] = high
        dh_lo[rows] = (dh - high.astype(F32)).astype(BF)
        return carry

    lax.fori_loop(0, ALL // 384, first, 0)

    def second(i, carry):
        rows = pl.ds(pl.multiple_of(i * 384, 384), 384)
        order = perm[rows]
        dh = nn(order, dh_hi[...]) + nn(order, dh_lo[...])
        g, u = gate[rows], upper[rows]
        sigma = jax.nn.sigmoid(g)
        active = g * sigma
        hidden = active * u
        meta = x[0, rows, 0:META].astype(F32)
        lane = lax.broadcasted_iota(jnp.int32, meta.shape, 1)
        named = jnp.where((meta == expert) & (lane < TOP), 1.0, 0.0)
        weight = pltpu.roll(meta, META - 8, 1) + (
            pltpu.roll(meta, META - 16, 1) + pltpu.roll(meta, META - 24, 1)
        )
        w = jnp.sum(named * weight, axis=1, keepdims=True)
        dc = jnp.sum(hidden * dh, axis=1, keepdims=True)
        ym[0, rows] = (named * dc).astype(BF)
        hid[rows] = (hidden * w).astype(BF)
        dh = dh * w
        dgate[rows] = (dh * u * sigma * (1.0 + g * (1.0 - sigma))).astype(BF)
        dup[rows] = (dh * active).astype(BF)
        return carry

    lax.fori_loop(0, ALL // 384, second, 0)

    def store(ref, rows, value):
        for q in range(Q):
            for t in range(2):
                start = t * HALF + q * PART
                ref[q, rows, t * PART : (t + 1) * PART] = value[:, start : start + PART]

    def third(i, carry):
        rows = pl.ds(pl.multiple_of(i * 384, 384), 384)
        order = perm[rows]
        store(y_v, rows, nn(hid[rows], vd[l]).astype(BF))
        a = nn(order, dgate[...]).astype(BF)
        b = nn(order, dup[...]).astype(BF)
        hid_c[rows] = nn(order, hid[...]).astype(BF)
        store(dx_v, rows, (nt(a, vg[l]) + nt(b, vu[l])).astype(BF))
        return carry

    lax.fori_loop(0, ALL // 384, third, 0)
    leaving = [
        pltpu.make_async_copy(held, out.at[:, l], out_sem.at[i]) for i, (held, out) in enumerate(((y_v, y), (dx_v, dx)))
    ]
    for copy in leaving:
        copy.start()

    def fourth(i, carry):
        cols = pl.ds(pl.multiple_of(i * 1024, 1024), 1024)
        own = x[0, :, pl.ds(pl.multiple_of(META + i * 1024, 128), 1024)]
        gg[0, cols] = tn(own, dgate[...]).astype(BF)
        gu[0, cols] = tn(own, dup[...]).astype(BF)
        gd[0, :, cols] = tn(hid_c[...], dy[0, :, cols]).astype(BF)
        return carry

    lax.fori_loop(0, D // 1024, fourth, 0)
    for copy in leaving:
        copy.wait()


def experts(old_layout, pair_moves, x, dy, perm, wg, wu, wd, wg_new, wu_new, wd_new):
    def block(*shape):
        return pl.BlockSpec((1, *shape), lambda l: (l,) + (0,) * len(shape))

    parts = pltpu.VMEM((Q, ALL, 2 * PART), BF)
    small = pltpu.VMEM((ALL, FF), BF)
    wide = pltpu.VMEM((ALL, FF), F32)
    return pl.pallas_call(
        expert_kernel,
        name="experts",
        grid=(2,),
        out_shape=(
            jax.ShapeDtypeStruct((Q, 2, ALL, 2 * PART), BF),
            jax.ShapeDtypeStruct((2, ALL, META), BF),
            jax.ShapeDtypeStruct((Q, 2, ALL, 2 * PART), BF),
            jax.ShapeDtypeStruct((2, D, FF), BF),
            jax.ShapeDtypeStruct((2, D, FF), BF),
            jax.ShapeDtypeStruct((2, FF, D), BF),
        ),
        in_specs=[
            pl.BlockSpec(memory_space=pltpu.SMEM), pl.BlockSpec(memory_space=pltpu.SMEM),
            block(ALL, WIDE), block(ALL, D),
            pl.BlockSpec((ALL, ALL), lambda l: (0, 0), pipeline_mode=pl.Buffered(1)),
            ANY, ANY, ANY, ANY, ANY, ANY,
        ],
        out_specs=[ANY, block(ALL, META), ANY, block(D, FF), block(D, FF), block(FF, D)],
        scratch_shapes=[
            parts, parts, pltpu.VMEM((2, D, FF), BF), pltpu.VMEM((2, D, FF), BF), pltpu.VMEM((2, FF, D), BF),
            wide, wide, small, small, small, small, small, small, small, small,
            pltpu.SemaphoreType.DMA((2, 3)), pltpu.SemaphoreType.DMA((2,)),
        ],
        compiler_params=pltpu.CompilerParams(
            dimension_semantics=("arbitrary",), vmem_limit_bytes=LIMIT
        ),
    )(old_layout, pair_moves, x, dy, perm, wg, wu, wd, wg_new, wu_new, wd_new)


def return_kernel(
    y_ref, ym_ref, dx_ref, st_tok, st_cot,
    mixed, d_tokens, d_combine,
    c_tok, c_meta, c_cot, raw_tok, raw_cot, s_tok, s_cot, m_tok, m_meta, m_cot,
    h_tok, h_meta, h_cot, rx_tok, rx_meta, rx_cot, xs_tok, xs_meta, xs_cot, ra_tok, ra_meta, ra_cot,
    a_send, a_recv, h_send, h_recv, x_send, x_recv, f_send, f_recv, loc_sem, st_sem,
):
    at = position()
    xlo, y, z, c, xhi = at["xlo"], at["y"], at["z"], at["c"], at["xhi"]
    near = ({"xlo": 1 - xlo}, {"xlo": 1 - xlo, "xhi": 1 - xhi})
    their_t = (xhi, 1 - xhi)
    greet([*near, *others("z", z * 2 + c), *others("y", y * 2 + c)])

    tok = (0, y_ref, c_tok, s_tok, m_tok, h_tok, rx_tok, xs_tok, ra_tok, "z", z * 2 + c, "y", y)
    cot = (1, dx_ref, c_cot, s_cot, m_cot, h_cot, rx_cot, xs_cot, ra_cot, "y", y * 2 + c, "z", z)
    small = (2, ym_ref, c_meta, s_tok, m_meta, h_meta, rx_meta, xs_meta, ra_meta, "z", z * 2 + c, "y", y)

    def exchange(side, q, j, slot):
        p, source, held, s, m, h, rx, xs, ra, axis, me, other, a = side
        return remote(
            source.at[q, :, j], held.at[q, slot], a_send.at[p, q, j], a_recv.at[p, q, slot],
            {axis: j // 2, "c": lax.rem(j, 2)},
        )

    def own(side, q):
        p, source, held, s, m, h, rx, xs, ra, axis, me, other, a = side
        return pltpu.make_async_copy(source.at[q, :, me], held.at[q, me], loc_sem.at[p, q])

    def relay(side, q, k):
        p, source, held, s, m, h, rx, xs, ra, axis, me, other, a = side
        piece = m.at[q, xlo, 0 if p == 2 else 1 - xhi, pl.ds(2 * k, 2)]
        return remote(piece, h.at[q, k], h_send.at[p, q, k], h_recv.at[p, q, k], near[k])

    def spread(side, q, k):
        p, source, held, s, m, h, rx, xs, ra, axis, me, other, a = side
        piece = m.at[q, 1 - xlo, k if p == 2 else their_t[k]]
        return remote(piece, rx.at[q, k], x_send.at[p, q, k], x_recv.at[p, q, k], near[k])

    def fold(side, q, k, slot):
        p, source, held, s, m, h, rx, xs, ra, axis, me, other, a = side
        to = lax.rem(a + k, 4)
        return remote(xs.at[q, to], ra.at[q, slot], f_send.at[p, q, k], f_recv.at[p, q, k], {other: to})

    def begin(side, q):
        def send(i, carry):
            exchange(side, q, lax.rem(side[10] + i, 8), side[10]).start()
            return carry

        lax.fori_loop(1, 8, send, 0)
        own(side, q).start()

    def begin_part(q, carry):
        begin(tok, q)
        begin(cot, q)
        return carry

    begin(small, 0)
    lax.fori_loop(0, Q, begin_part, 0)
    loads = [
        pltpu.make_async_copy(src, raw, st_sem.at[i]) for i, (src, raw) in enumerate(((st_tok, raw_tok), (st_cot, raw_cot)))
    ]
    for load in loads:
        load.start()
    for load, raw, s in ((loads[0], raw_tok, s_tok), (loads[1], raw_cot, s_cot)):
        load.wait()
        for g in range(2):

            def turn(n, carry, raw=raw, s=s, g=g):
                cols = pl.ds(pl.multiple_of(n * 128, 128), 128)
                s[g, cols] = raw[g, :, cols].astype(F32).T.astype(BF)
                return carry

            lax.fori_loop(0, SPAN // 128, turn, 0)

    def combine(side, q):
        p, source, held, s, m, h, rx, xs, ra, axis, me, other, a = side

        def arrive(i, carry):
            j = lax.rem(me + i, 8)
            exchange(side, q, j, j).wait_recv()
            return carry

        lax.fori_loop(1, 8, arrive, 0)
        own(side, q).wait()
        size = held.shape[-1]
        for g in range(2):
            part = held[q, :, :, g * GROUP : (g + 1) * GROUP].reshape(ALL, size)
            got = jnp.dot(s[g], part, preferred_element_type=F32).astype(BF)
            if p == 2:
                for t in range(2):
                    m[q, g, t] = got.reshape(4, TOK, META)
            else:
                for t in range(2):
                    m[q, g, t] = got[:, t * PART : (t + 1) * PART].reshape(4, TOK, PART)
        for k in range(2):
            relay(side, q, k).start()

    def pass_on(side, q):
        p, source, held, s, m, h, rx, xs, ra, axis, me, other, a = side
        for k in range(2):
            relay(side, q, k).wait_recv()
            t = (1 - k) if p == 2 else their_t[1 - k]
            half = pl.ds(2 * k, 2)
            total = m[q, 1 - xlo, t, half].astype(F32) + h[q, k].astype(F32)
            m[q, 1 - xlo, t, half] = total.astype(BF)
        for k in range(2):
            spread(side, q, k).start()

    def gather(side, q):
        p, source, held, s, m, h, rx, xs, ra, axis, me, other, a = side
        for k in range(2):
            spread(side, q, k).wait_recv()
        total = m[q, xlo, 0 if p == 2 else xhi].astype(F32)
        for k in range(2):
            total = total + rx[q, k].astype(F32)
        xs[q] = total.astype(BF)
        for k in range(1, 4):
            fold(side, q, k, a).start()

    def close(side, q):
        p, source, held, s, m, h, rx, xs, ra, axis, me, other, a = side
        for k in range(1, 4):
            fold(side, q, k, a).wait_recv()
        total = xs[q, a].astype(F32)
        for k in range(1, 4):
            total = total + ra[q, lax.rem(a + k, 4)].astype(F32)
        if p == 2:
            d_combine[...] = total.T[0:TOP]
        else:
            (mixed, d_tokens)[p][:, pl.ds(pl.multiple_of(q * PART, PART), PART)] = total.astype(BF)
        for k in range(2):
            relay(side, q, k).wait_send()
            spread(side, q, k).wait_send()
            fold(side, q, k + 1, a).wait_send()
        fold(side, q, 3, a).wait_send()

        def sent(i, carry):
            exchange(side, q, lax.rem(me + i, 8), me).wait_send()
            return carry

        lax.fori_loop(1, 8, sent, 0)

    def both(stage, q):
        stage(tok, q)
        stage(cot, q)

    combine(small, 0)
    both(combine, 0)
    pass_on(small, 0)
    both(pass_on, 0)
    both(combine, 1)
    gather(small, 0)
    both(gather, 0)
    both(pass_on, 1)

    def flow(q, carry):
        both(combine, q)
        both(gather, q - 1)
        both(pass_on, q)
        both(close, q - 2)
        return carry

    lax.fori_loop(2, Q, flow, 0)
    close(small, 0)
    both(gather, Q - 1)
    both(close, Q - 2)
    both(close, Q - 1)


def give_back(y, ym, dx, st_tok, st_cot):
    dma = pltpu.SemaphoreType.DMA

    def each(*shape):
        return [
            pltpu.VMEM((Q, *shape, PART), BF), pltpu.VMEM((1, *shape, META), BF), pltpu.VMEM((Q, *shape, PART), BF)
        ]

    held = (8, 2, ROWS)
    return pl.pallas_call(
        return_kernel,
        name="give_back",
        out_shape=(
            jax.ShapeDtypeStruct((TOK, HALF), BF),
            jax.ShapeDtypeStruct((TOK, HALF), BF),
            jax.ShapeDtypeStruct((TOP, TOK), F32),
        ),
        in_specs=[ANY] * 5,
        out_specs=[VMEM] * 3,
        scratch_shapes=[
            pltpu.VMEM((Q, *held, 2 * PART), BF), pltpu.VMEM((1, *held, META), BF), pltpu.VMEM((Q, *held, 2 * PART), BF),
            pltpu.VMEM((2, ALL, SPAN), BF), pltpu.VMEM((2, ALL, SPAN), BF),
            pltpu.VMEM((2, SPAN, ALL), BF), pltpu.VMEM((2, SPAN, ALL), BF),
            *each(2, 2, 4, TOK), *each(2, 2, TOK), *each(2, 4, TOK), *each(4, TOK), *each(4, TOK),
            dma((3, Q, 8)), dma((3, Q, 8)), dma((3, Q, 2)), dma((3, Q, 2)), dma((3, Q, 2)), dma((3, Q, 2)),
            dma((3, Q, 4)), dma((3, Q, 4)), dma((3, Q)), dma((2,)),
        ],
        compiler_params=pltpu.CompilerParams(
            collective_id=1, has_side_effects=True, vmem_limit_bytes=LIMIT
        ),
    )(y, ym, dx, st_tok, st_cot)


def hand_over_kernel(a, b, c, a_out, b_out, c_out):
    a_out[...] = a[...]
    b_out[...] = b[...]
    c_out[...] = c[...]


def hand_over(*values):
    return pl.pallas_call(
        hand_over_kernel,
        name="hand_over",
        out_shape=tuple(jax.ShapeDtypeStruct(v.shape, v.dtype) for v in values),
        in_specs=[VMEM] * 3,
        out_specs=[VMEM] * 3,
    )(*values)


def body(tokens, expert_ids, combine, cotangent, old_layout, pair_moves, gate_w, up_w, down_w):
    x, dy, st_tok, st_cot, wg_new, wu_new, wd_new, perm = dispatch(
        tokens, cotangent, expert_ids.T, combine.T, old_layout, pair_moves, gate_w, up_w, down_w
    )
    y_rows, y_meta, dx_rows, gg, gu, gd = experts(
        old_layout, pair_moves, x.reshape(2, ALL, WIDE), dy.reshape(2, ALL, D), perm,
        gate_w, up_w, down_w, wg_new, wu_new, wd_new,
    )
    mixed, d_tokens, d_combine = give_back(
        y_rows.reshape(Q, 2, 8, ROWS, 2 * PART), y_meta.reshape(1, 2, 8, ROWS, META),
        dx_rows.reshape(Q, 2, 8, ROWS, 2 * PART), st_tok, st_cot,
    )
    mixed, d_tokens, d_combine = hand_over(mixed, d_tokens, d_combine)
    return mixed, d_tokens, d_combine.T, gg, gu, gd


def solution(mesh):
    fine = Mesh(mesh.devices.reshape(2, 4, 4, 2, 2), (*EP, "xhi"))
    return jax.shard_map(
        body,
        mesh=fine,
        in_specs=(
            P(EP, None), P(EP, None), P(EP, None), P(EP, None), P(), P(),
            P(EP, None, "xhi"), P(EP, None, "xhi"), P(EP, "xhi", None),
        ),
        out_specs=(
            P(EP, "xhi"), P(EP, "xhi"), P(EP, None),
            P(EP, None, "xhi"), P(EP, None, "xhi"), P(EP, "xhi", None),
        ),
        check_vma=False,
    )
```

```python
import jax
import jax.numpy as jnp
from jax import lax
from jax.experimental import pallas as pl
from jax.experimental.pallas import tpu as pltpu
from jax.sharding import Mesh, PartitionSpec as P

MESH = pl.DeviceIdType.MESH
BF, F32 = jnp.bfloat16, jnp.float32
D, FF, CAP, TOK, TOP = 2048, 384, 12, 128, 8
META = 128
WIDE = META + D
BLOCKS = 8
GROUP, SPAN = 4 * CAP, 4 * TOK
ROWS = BLOCKS * CAP
ALL = BLOCKS * ROWS
HALF = D // 2
Q = 4
PART = HALF // Q
LIMIT = 66 * 1024 * 1024 - 4096
EP = ("xlo", "z", "y", "c")
ANY = pl.BlockSpec(memory_space=pl.ANY)
VMEM = pl.BlockSpec(memory_space=pltpu.VMEM)


def position():
    return {name: lax.axis_index(name) for name in ("xlo", "z", "y", "c", "xhi")}


def greet(devices):
    barrier = pltpu.get_barrier_semaphore()
    for device in devices:
        pl.semaphore_signal(barrier, inc=1, device_id=device, device_id_type=MESH)
    pl.semaphore_wait(barrier, len(devices))


def remote(source, target, send, recv, device):
    return pltpu.make_async_remote_copy(
        src_ref=source,
        dst_ref=target,
        send_sem=send,
        recv_sem=recv,
        device_id=device,
        device_id_type=MESH,
    )


def others(axis, me):
    found = []
    for step in range(1, 8):
        j = lax.rem(me + step, 8)
        found.append({axis: j // 2, "c": lax.rem(j, 2)})
    return found


def expert_at(old_layout, pair_moves, device, l):
    if l == 0:
        return old_layout[device * 2]
    source = jnp.where(pair_moves[device] == 1, lax.rem(device + 32, 64), device)
    return old_layout[source * 2 + 1]


def dispatch_kernel(
    tok_ref, cot_ref, ids_ref, combine_ref, old_layout, pair_moves, wg, wu, wd,
    x_out, dy_out, st_tok_out, st_cot_out, wg_out, wu_out, wd_out, perm_out,
    g0_tok, g1_tok, g0_cot, g1_cot, sel0_tok, sel1_tok, sel0_cot, sel1_cot,
    st_tok, st_cot, code_tok, code_cot, e_tok, e_cot, rowcode, upper, perm,
    ag_send, ag_recv, x_send, x_recv, st_sem, in_sem, loc_sem, w_send, w_recv,
):
    at = position()
    xlo, y, z, c, xhi = at["xlo"], at["y"], at["z"], at["c"], at["xhi"]
    direct, flipped = {"xlo": 1 - xlo}, {"xlo": 1 - xlo, "xhi": 1 - xhi}
    me_z, me_y = z * 2 + c, y * 2 + c

    gathers = (
        (0, tok_ref, (g0_tok, g1_tok), "y", y),
        (1, cot_ref, (g0_cot, g1_cot), "z", z),
    )

    def load(side, h):
        p, source, gathered, axis, a = side
        target = gathered[h].at[xlo * 4 + a]
        if h == 0:
            target = target.at[:, META : META + HALF]
        return pltpu.make_async_copy(source.at[:, h * HALF : (h + 1) * HALF], target, in_sem.at[p, h])

    for h in range(2):
        for side in gathers:
            load(side, h).start()
    w = combine_ref[...]
    high = w.astype(BF).astype(F32)
    middle = (w - high).astype(BF).astype(F32)
    facts = jnp.concatenate(
        [ids_ref[...].astype(F32), high, middle, w - high - middle, jnp.zeros((META - 32, TOK), F32)], axis=0
    )
    meta = facts.T.astype(BF)
    for p, source, gathered, axis, a in gathers:
        gathered[0][xlo * 4 + a, :, 0:META] = meta
    greet([direct, flipped] + others("z", me_z) + others("y", me_y))

    def copies(side, h):
        p, source, gathered, axis, a = side
        held = gathered[h]
        right, left = {axis: lax.rem(a + 1, 4)}, {axis: lax.rem(a + 3, 4)}
        opposite = lax.rem(a + 2, 4)
        mine, theirs = xlo * 4, (1 - xlo) * 4
        l, r = lax.rem(a + 3, 4), lax.rem(a + 1, 4)
        lo, hi = pl.ds(0, 64), pl.ds(64, 64)
        own = held.at[mine + a]
        plan = [
            (own, flipped, held.at[theirs + a]),
            (own, right, held.at[mine + l]),
            (own, left, held.at[mine + r]),
            (held.at[theirs + a], right, held.at[theirs + l]),
            (held.at[theirs + a], left, held.at[theirs + r]),
            (held.at[mine + l, lo], right, held.at[mine + opposite, lo]),
            (held.at[theirs + l, lo], right, held.at[theirs + opposite, lo]),
            (held.at[mine + r, hi], left, held.at[mine + opposite, hi]),
            (held.at[theirs + r, hi], left, held.at[theirs + opposite, hi]),
        ]
        out = [remote(t, t, ag_send.at[p, h, i], ag_recv.at[p, h, i], dev) for i, (t, dev, _) in enumerate(plan)]
        come = [remote(t, got, ag_send.at[p, h, i], ag_recv.at[p, h, i], dev) for i, (t, dev, got) in enumerate(plan)]
        return out, come

    moves = [[copies(side, h) for side in gathers] for h in range(2)]

    def open_half(h):
        for side, (out, _) in zip(gathers, moves[h]):
            load(side, h).wait()
            for i in (1, 2, 0):
                out[i].start()

    def pass_half(h, arrival, starts):
        for out, come in moves[h]:
            come[arrival].wait_recv()
            for i in starts:
                out[i].start()

    def close_half(h):
        for out, come in moves[h]:
            for i in (5, 6, 7, 8):
                come[i].wait_recv()

    open_half(0)
    weights = [
        remote(src.at[1], dst, w_send.at[i], w_recv.at[i], direct)
        for i, (src, dst) in enumerate(((wg, wg_out), (wu, wu_out), (wd, wd_out)))
    ]
    for copy in weights:
        copy.start()

    row = lax.broadcasted_iota(jnp.int32, (GROUP, SPAN), 0)
    col = lax.broadcasted_iota(jnp.int32, (GROUP, SPAN), 1)
    value = jnp.full((GROUP, SPAN), -2, jnp.int32)
    for b in range(4):
        inside = (row >= b * CAP) & (row < (b + 1) * CAP) & (col >= b * TOK) & (col < (b + 1) * TOK)
        value = jnp.where(inside, row - b * CAP, value)
    rowcode[...] = value.astype(F32)
    before = lax.broadcasted_iota(jnp.int32, (TOK, TOK), 0) < lax.broadcasted_iota(jnp.int32, (TOK, TOK), 1)
    upper[...] = jnp.where(before, 1.0, 0.0).astype(BF)
    place = lax.broadcasted_iota(jnp.int32, (16, TOK), 0)
    along_z, along_y = jnp.zeros((16, TOK), jnp.int32), jnp.zeros((16, TOK), jnp.int32)
    for slot in range(16):
        b, core, l = slot // 4, slot // 2 % 2, slot % 2
        found = expert_at(old_layout, pair_moves, ((xlo * 4 + b) * 4 + y) * 2 + core, l)
        along_z = jnp.where(place == slot, found, along_z)
        found = expert_at(old_layout, pair_moves, ((xlo * 4 + z) * 4 + b) * 2 + core, l)
        along_y = jnp.where(place == slot, found, along_y)
    e_tok[...] = along_z.astype(F32)
    e_cot[...] = along_y.astype(F32)

    pass_half(0, 0, (3, 4))
    pass_half(0, 1, (5,))
    pass_half(0, 2, (7,))
    open_half(1)

    def strip(i, carry):
        lr = lax.broadcasted_iota(jnp.int32, (GROUP, ALL), 0)
        lc = lax.broadcasted_iota(jnp.int32, (GROUP, ALL), 1)
        inner = jnp.where(lr >= 12, 1, 0) + jnp.where(lr >= 24, 1, 0) + jnp.where(lr >= 36, 1, 0)
        there = i * GROUP + lr + (2 * ROWS - CAP) * (inner - i // 4)
        perm[pl.ds(pl.multiple_of(i * GROUP, GROUP), GROUP)] = jnp.where(lc == there, 1.0, 0.0).astype(BF)
        return carry

    lax.fori_loop(0, ALL // GROUP, strip, 0)
    perm_copy = pltpu.make_async_copy(perm, perm_out, loc_sem.at[4])
    perm_copy.start()
    pass_half(0, 3, (6,))
    pass_half(0, 4, (8,))
    close_half(0)

    def choose(gathered, experts, code, st):
        for b in range(BLOCKS):
            ids = gathered[b, :, 0:META].astype(F32).T[0:TOP]
            member = jnp.zeros((16, TOK), F32)
            for k in range(TOP):
                member = member + jnp.where(ids[k : k + 1] == experts[...], 1.0, 0.0)
            place = jnp.dot(member.astype(BF), upper[...], preferred_element_type=F32)
            found = jnp.where(member > 0.5, place, -1.0)
            for d in range(8):
                code[d, 0:2, b * TOK : (b + 1) * TOK] = found[2 * d : 2 * d + 2]

        def fill(d, carry):
            rows = code[d]
            for g in range(2):
                for l in range(2):
                    wanted = rows[l : l + 1, g * SPAN : (g + 1) * SPAN]
                    to = pl.ds(pl.multiple_of(d * 2 * GROUP + l * GROUP, GROUP), GROUP)
                    st[g, to] = jnp.where(rowcode[...] == wanted, 1.0, 0.0).astype(BF)
            return carry

        lax.fori_loop(0, 8, fill, 0)

    def emit(pair, gathered, start, sel, st):
        width = sel.shape[-1]
        from_rows = pl.ds(pl.multiple_of(pair * 4 * GROUP, 4 * GROUP), 4 * GROUP)
        for g in range(2):
            source = gathered[g * 4 : (g + 1) * 4, :, start : start + width].reshape(SPAN, width)
            got = jnp.dot(st[g, from_rows], source, preferred_element_type=F32).astype(BF)
            sel[pl.ds(pair * 2, 2), :, g * GROUP : (g + 1) * GROUP] = got.reshape(2, 2, GROUP, width)

    sides = (
        (0, (g0_tok, g1_tok), e_tok, code_tok, (sel0_tok, sel1_tok), st_tok, st_tok_out, x_out, "z", z, (0, META + HALF)),
        (1, (g0_cot, g1_cot), e_cot, code_cot, (sel0_cot, sel1_cot), st_cot, st_cot_out, dy_out, "y", y, (0, HALF)),
    )

    def target(side, h, slot):
        out, sel, start = side[7], side[4][h], side[10][h]
        return out.at[:, slot, :, pl.ds(start, sel.shape[-1])]

    def exchange(side, h, j, slot):
        p, sel, axis = side[0], side[4][h], side[8]
        return remote(
            sel.at[j], target(side, h, slot), x_send.at[p, h, j], x_recv.at[p, h, slot],
            {axis: j // 2, "c": lax.rem(j, 2)},
        )

    def keep(side, h):
        j = side[9] * 2 + c
        return pltpu.make_async_copy(side[4][h].at[j], target(side, h, j), loc_sem.at[2 * side[0] + h])

    def produce(h, i):
        for side in sides:
            p, gathered, experts, code, sel, st, st_out, out, axis, b, starts = side
            pair = lax.rem(b + i, 4)
            skip = META if h == 0 and p == 1 else 0
            emit(pair, gathered[h], skip, sel[h], st)
            if i < 4:
                for core in range(2):
                    exchange(side, h, pair * 2 + core, b * 2 + c).start()
            else:
                exchange(side, h, b * 2 + 1 - c, b * 2 + c).start()
                keep(side, h).start()

    for side in sides:
        p, gathered, experts, code, sel, st, st_out, out, axis, b, starts = side
        choose(gathered[0], experts, code, st)
        pltpu.make_async_copy(st, st_out, st_sem.at[p]).start()
        if p == 0:
            pass_half(1, 0, (3, 4))
    produce(0, 1)
    pass_half(1, 1, (5,))
    pass_half(1, 2, (7,))
    produce(0, 2)
    pass_half(1, 3, (6,))
    pass_half(1, 4, (8,))
    produce(0, 3)
    produce(0, 4)
    close_half(1)
    for i in range(1, 5):
        produce(1, i)

    for h in range(2):

        def finish(i, carry):
            for side in sides:
                j = lax.rem(side[9] * 2 + c + i, 8)
                exchange(side, h, j, j).wait_send()
                exchange(side, h, j, j).wait_recv()
            return carry

        lax.fori_loop(1, 8, finish, 0)
        for side in sides:
            keep(side, h).wait()
        for out, _ in moves[h]:
            for copy in out:
                copy.wait_send()
    for side in sides:
        pltpu.make_async_copy(side[5], side[6], st_sem.at[side[0]]).wait()
    perm_copy.wait()
    for copy in weights:
        copy.wait()


def dispatch(tok, cot, ids, combine, old_layout, pair_moves, wg, wu, wd):
    choice = pltpu.VMEM((2, ALL, SPAN), BF)
    code = pltpu.VMEM((8, 8, BLOCKS * TOK), F32)
    dma = pltpu.SemaphoreType.DMA
    smem = pl.BlockSpec(memory_space=pltpu.SMEM)
    halves = [pltpu.VMEM((BLOCKS, TOK, META + HALF), BF), pltpu.VMEM((BLOCKS, TOK, HALF), BF)]
    wide, narrow = pltpu.VMEM((8, 2, ROWS, META + HALF), BF), pltpu.VMEM((8, 2, ROWS, HALF), BF)
    return pl.pallas_call(
        dispatch_kernel,
        name="dispatch",
        out_shape=(
            jax.ShapeDtypeStruct((2, 8, ROWS, WIDE), BF),
            jax.ShapeDtypeStruct((2, 8, ROWS, D), BF),
            jax.ShapeDtypeStruct((2, ALL, SPAN), BF),
            jax.ShapeDtypeStruct((2, ALL, SPAN), BF),
            jax.ShapeDtypeStruct((D, FF), BF),
            jax.ShapeDtypeStruct((D, FF), BF),
            jax.ShapeDtypeStruct((FF, D), BF),
            jax.ShapeDtypeStruct((ALL, ALL), BF),
        ),
        in_specs=[ANY, ANY, VMEM, VMEM, smem, smem, ANY, ANY, ANY],
        out_specs=[ANY] * 8,
        scratch_shapes=[
            *halves, *halves, wide, narrow, narrow, narrow,
            choice, choice, code, code, pltpu.VMEM((16, TOK), F32), pltpu.VMEM((16, TOK), F32),
            pltpu.VMEM((GROUP, SPAN), F32), pltpu.VMEM((TOK, TOK), BF), pltpu.VMEM((ALL, ALL), BF),
            dma((2, 2, 9)), dma((2, 2, 9)), dma((2, 2, 8)), dma((2, 2, 8)), dma((2,)), dma((2, 2)), dma((5,)),
            dma((3,)), dma((3,)),
        ],
        compiler_params=pltpu.CompilerParams(
            collective_id=0, has_side_effects=True, vmem_limit_bytes=LIMIT
        ),
    )(tok, cot, ids, combine, old_layout, pair_moves, wg, wu, wd)


def expert_kernel(
    old_layout, pair_moves, x, dy, perm, wg, wu, wd, wg_new, wu_new, wd_new,
    y, ym, dx, gg, gu, gd,
    y_v, dx_v, vg, vu, vd, gate, upper, dh_hi, dh_lo, hid, dgate, dup, hid_c, dgate_c, dup_c, sem, out_sem,
):
    l = pl.program_id(0)
    at = position()
    device = ((at["xlo"] * 4 + at["z"]) * 4 + at["y"]) * 2 + at["c"]
    moved = pair_moves[device] == 1
    pairs = ((wg, wg_new, vg), (wu, wu_new, vu), (wd, wd_new, vd))

    @pl.when(l == 0)
    def _():
        for i, (old, new, held) in enumerate(pairs):
            pltpu.make_async_copy(old.at[0], held.at[0], sem.at[0, i]).start()
        for i, (old, new, held) in enumerate(pairs):

            @pl.when(moved)
            def _(new=new, held=held, i=i):
                pltpu.make_async_copy(new, held.at[1], sem.at[1, i]).start()

            @pl.when(jnp.logical_not(moved))
            def _(old=old, held=held, i=i):
                pltpu.make_async_copy(old.at[1], held.at[1], sem.at[1, i]).start()

    for i, (old, new, held) in enumerate(pairs):
        pltpu.make_async_copy(old.at[0], held.at[l], sem.at[l, i]).wait()
    expert = jnp.where(
        l == 0, expert_at(old_layout, pair_moves, device, 0), expert_at(old_layout, pair_moves, device, 1)
    ).astype(F32)

    def nt(a, b):
        return lax.dot_general(a, b, (((1,), (1,)), ((), ())), preferred_element_type=F32)

    def tn(a, b):
        return lax.dot_general(a, b, (((0,), (0,)), ((), ())), preferred_element_type=F32)

    def nn(a, b):
        return jnp.dot(a, b, preferred_element_type=F32)

    def first(i, carry):
        rows = pl.ds(pl.multiple_of(i * 384, 384), 384)
        own = x[0, rows, META:WIDE]
        gate[rows] = nn(own, vg[l])
        upper[rows] = nn(own, vu[l])
        dh = nt(dy[0, rows], vd[l])
        high = dh.astype(BF)
        dh_hi[rows] = high
        dh_lo[rows] = (dh - high.astype(F32)).astype(BF)
        return carry

    lax.fori_loop(0, ALL // 384, first, 0)

    def second(i, carry):
        rows = pl.ds(pl.multiple_of(i * 384, 384), 384)
        order = perm[rows]
        dh = nn(order, dh_hi[...]) + nn(order, dh_lo[...])
        g, u = gate[rows], upper[rows]
        sigma = jax.nn.sigmoid(g)
        active = g * sigma
        hidden = active * u
        meta = x[0, rows, 0:META].astype(F32)
        lane = lax.broadcasted_iota(jnp.int32, meta.shape, 1)
        named = jnp.where((meta == expert) & (lane < TOP), 1.0, 0.0)
        weight = pltpu.roll(meta, META - 8, 1) + (
            pltpu.roll(meta, META - 16, 1) + pltpu.roll(meta, META - 24, 1)
        )
        w = jnp.sum(named * weight, axis=1, keepdims=True)
        dc = jnp.sum(hidden * dh, axis=1, keepdims=True)
        ym[0, rows] = (named * dc).astype(BF)
        hid[rows] = (hidden * w).astype(BF)
        dh = dh * w
        dgate[rows] = (dh * u * sigma * (1.0 + g * (1.0 - sigma))).astype(BF)
        dup[rows] = (dh * active).astype(BF)
        return carry

    lax.fori_loop(0, ALL // 384, second, 0)

    def store(ref, rows, value):
        for q in range(Q):
            for t in range(2):
                start = t * HALF + q * PART
                ref[q, rows, t * PART : (t + 1) * PART] = value[:, start : start + PART]

    def third(i, carry):
        rows = pl.ds(pl.multiple_of(i * 768, 768), 768)
        order = perm[rows]
        store(y_v, rows, nn(hid[rows], vd[l]).astype(BF))
        a = nn(order, dgate[...]).astype(BF)
        b = nn(order, dup[...]).astype(BF)
        hid_c[rows] = nn(order, hid[...]).astype(BF)
        store(dx_v, rows, (nt(a, vg[l]) + nt(b, vu[l])).astype(BF))
        return carry

    lax.fori_loop(0, ALL // 768, third, 0)
    leaving = [
        pltpu.make_async_copy(held, out.at[:, l], out_sem.at[i]) for i, (held, out) in enumerate(((y_v, y), (dx_v, dx)))
    ]
    for copy in leaving:
        copy.start()

    def fourth(i, carry):
        cols = pl.ds(pl.multiple_of(i * 1024, 1024), 1024)
        own = x[0, :, pl.ds(pl.multiple_of(META + i * 1024, 128), 1024)]
        gg[0, cols] = tn(own, dgate[...]).astype(BF)
        gu[0, cols] = tn(own, dup[...]).astype(BF)
        gd[0, :, cols] = tn(hid_c[...], dy[0, :, cols]).astype(BF)
        return carry

    lax.fori_loop(0, D // 1024, fourth, 0)
    for copy in leaving:
        copy.wait()


def experts(old_layout, pair_moves, x, dy, perm, wg, wu, wd, wg_new, wu_new, wd_new):
    def block(*shape):
        return pl.BlockSpec((1, *shape), lambda l: (l,) + (0,) * len(shape))

    parts = pltpu.VMEM((Q, ALL, 2 * PART), BF)
    small = pltpu.VMEM((ALL, FF), BF)
    wide = pltpu.VMEM((ALL, FF), F32)
    return pl.pallas_call(
        expert_kernel,
        name="experts",
        grid=(2,),
        out_shape=(
            jax.ShapeDtypeStruct((Q, 2, ALL, 2 * PART), BF),
            jax.ShapeDtypeStruct((2, ALL, META), BF),
            jax.ShapeDtypeStruct((Q, 2, ALL, 2 * PART), BF),
            jax.ShapeDtypeStruct((2, D, FF), BF),
            jax.ShapeDtypeStruct((2, D, FF), BF),
            jax.ShapeDtypeStruct((2, FF, D), BF),
        ),
        in_specs=[
            pl.BlockSpec(memory_space=pltpu.SMEM), pl.BlockSpec(memory_space=pltpu.SMEM),
            block(ALL, WIDE), block(ALL, D),
            pl.BlockSpec((ALL, ALL), lambda l: (0, 0), pipeline_mode=pl.Buffered(1)),
            ANY, ANY, ANY, ANY, ANY, ANY,
        ],
        out_specs=[ANY, block(ALL, META), ANY, block(D, FF), block(D, FF), block(FF, D)],
        scratch_shapes=[
            parts, parts, pltpu.VMEM((2, D, FF), BF), pltpu.VMEM((2, D, FF), BF), pltpu.VMEM((2, FF, D), BF),
            wide, wide, small, small, small, small, small, small, small, small,
            pltpu.SemaphoreType.DMA((2, 3)), pltpu.SemaphoreType.DMA((2,)),
        ],
        compiler_params=pltpu.CompilerParams(
            dimension_semantics=("arbitrary",), vmem_limit_bytes=LIMIT
        ),
    )(old_layout, pair_moves, x, dy, perm, wg, wu, wd, wg_new, wu_new, wd_new)


def return_kernel(
    y_ref, ym_ref, dx_ref, st_tok, st_cot,
    mixed, d_tokens, d_combine,
    c_tok, c_meta, c_cot, raw_tok, raw_cot, s_tok, s_cot, m_tok, m_meta, m_cot,
    h_tok, h_meta, h_cot, rx_tok, rx_meta, rx_cot, xs_tok, xs_meta, xs_cot, ra_tok, ra_meta, ra_cot,
    a_send, a_recv, h_send, h_recv, x_send, x_recv, f_send, f_recv, loc_sem, st_sem,
):
    at = position()
    xlo, y, z, c, xhi = at["xlo"], at["y"], at["z"], at["c"], at["xhi"]
    near = ({"xlo": 1 - xlo}, {"xlo": 1 - xlo, "xhi": 1 - xhi})
    their_t = (xhi, 1 - xhi)
    greet([*near, *others("z", z * 2 + c), *others("y", y * 2 + c)])

    tok = (0, y_ref, c_tok, s_tok, m_tok, h_tok, rx_tok, xs_tok, ra_tok, "z", z * 2 + c, "y", y)
    cot = (1, dx_ref, c_cot, s_cot, m_cot, h_cot, rx_cot, xs_cot, ra_cot, "y", y * 2 + c, "z", z)
    small = (2, ym_ref, c_meta, s_tok, m_meta, h_meta, rx_meta, xs_meta, ra_meta, "z", z * 2 + c, "y", y)

    def exchange(side, q, j, slot):
        p, source, held, s, m, h, rx, xs, ra, axis, me, other, a = side
        return remote(
            source.at[q, :, j], held.at[q, slot], a_send.at[p, q, j], a_recv.at[p, q, slot],
            {axis: j // 2, "c": lax.rem(j, 2)},
        )

    def own(side, q):
        p, source, held, s, m, h, rx, xs, ra, axis, me, other, a = side
        return pltpu.make_async_copy(source.at[q, :, me], held.at[q, me], loc_sem.at[p, q])

    def relay(side, q, k):
        p, source, held, s, m, h, rx, xs, ra, axis, me, other, a = side
        piece = m.at[q, xlo, 0 if p == 2 else 1 - xhi, pl.ds(2 * k, 2)]
        return remote(piece, h.at[q, k], h_send.at[p, q, k], h_recv.at[p, q, k], near[k])

    def spread(side, q, k):
        p, source, held, s, m, h, rx, xs, ra, axis, me, other, a = side
        piece = m.at[q, 1 - xlo, k if p == 2 else their_t[k]]
        return remote(piece, rx.at[q, k], x_send.at[p, q, k], x_recv.at[p, q, k], near[k])

    def fold(side, q, k, slot):
        p, source, held, s, m, h, rx, xs, ra, axis, me, other, a = side
        to = lax.rem(a + k, 4)
        return remote(xs.at[q, to], ra.at[q, slot], f_send.at[p, q, k], f_recv.at[p, q, k], {other: to})

    def begin(side, q):
        def send(i, carry):
            exchange(side, q, lax.rem(side[10] + i, 8), side[10]).start()
            return carry

        lax.fori_loop(1, 8, send, 0)
        own(side, q).start()

    def begin_part(q, carry):
        begin(tok, q)
        begin(cot, q)
        return carry

    begin(small, 0)
    lax.fori_loop(0, Q, begin_part, 0)
    loads = [
        pltpu.make_async_copy(src, raw, st_sem.at[i]) for i, (src, raw) in enumerate(((st_tok, raw_tok), (st_cot, raw_cot)))
    ]
    for load in loads:
        load.start()
    for load, raw, s in ((loads[0], raw_tok, s_tok), (loads[1], raw_cot, s_cot)):
        load.wait()
        for g in range(2):

            def turn(n, carry, raw=raw, s=s, g=g):
                cols = pl.ds(pl.multiple_of(n * 128, 128), 128)
                s[g, cols] = raw[g, :, cols].astype(F32).T.astype(BF)
                return carry

            lax.fori_loop(0, SPAN // 128, turn, 0)

    def combine(side, q):
        p, source, held, s, m, h, rx, xs, ra, axis, me, other, a = side

        def arrive(i, carry):
            j = lax.rem(me + i, 8)
            exchange(side, q, j, j).wait_recv()
            return carry

        lax.fori_loop(1, 8, arrive, 0)
        own(side, q).wait()
        size = held.shape[-1]
        for g in range(2):
            part = held[q, :, :, g * GROUP : (g + 1) * GROUP].reshape(ALL, size)
            got = jnp.dot(s[g], part, preferred_element_type=F32).astype(BF)
            if p == 2:
                for t in range(2):
                    m[q, g, t] = got.reshape(4, TOK, META)
            else:
                for t in range(2):
                    m[q, g, t] = got[:, t * PART : (t + 1) * PART].reshape(4, TOK, PART)
        for k in range(2):
            relay(side, q, k).start()

    def pass_on(side, q):
        p, source, held, s, m, h, rx, xs, ra, axis, me, other, a = side
        for k in range(2):
            relay(side, q, k).wait_recv()
            t = (1 - k) if p == 2 else their_t[1 - k]
            half = pl.ds(2 * k, 2)
            total = m[q, 1 - xlo, t, half].astype(F32) + h[q, k].astype(F32)
            m[q, 1 - xlo, t, half] = total.astype(BF)
        for k in range(2):
            spread(side, q, k).start()

    def gather(side, q):
        p, source, held, s, m, h, rx, xs, ra, axis, me, other, a = side
        for k in range(2):
            spread(side, q, k).wait_recv()
        total = m[q, xlo, 0 if p == 2 else xhi].astype(F32)
        for k in range(2):
            total = total + rx[q, k].astype(F32)
        xs[q] = total.astype(BF)
        for k in range(1, 4):
            fold(side, q, k, a).start()

    def close(side, q):
        p, source, held, s, m, h, rx, xs, ra, axis, me, other, a = side
        for k in range(1, 4):
            fold(side, q, k, a).wait_recv()
        total = xs[q, a].astype(F32)
        for k in range(1, 4):
            total = total + ra[q, lax.rem(a + k, 4)].astype(F32)
        if p == 2:
            d_combine[...] = total.T[0:TOP]
        else:
            (mixed, d_tokens)[p][:, pl.ds(pl.multiple_of(q * PART, PART), PART)] = total.astype(BF)
        for k in range(2):
            relay(side, q, k).wait_send()
            spread(side, q, k).wait_send()
            fold(side, q, k + 1, a).wait_send()
        fold(side, q, 3, a).wait_send()

        def sent(i, carry):
            exchange(side, q, lax.rem(me + i, 8), me).wait_send()
            return carry

        lax.fori_loop(1, 8, sent, 0)

    def both(stage, q):
        stage(tok, q)
        stage(cot, q)

    combine(small, 0)
    both(combine, 0)
    pass_on(small, 0)
    both(pass_on, 0)
    both(combine, 1)
    gather(small, 0)
    both(gather, 0)
    both(pass_on, 1)

    def flow(q, carry):
        both(combine, q)
        both(gather, q - 1)
        both(pass_on, q)
        both(close, q - 2)
        return carry

    lax.fori_loop(2, Q, flow, 0)
    close(small, 0)
    both(gather, Q - 1)
    both(close, Q - 2)
    both(close, Q - 1)


def give_back(y, ym, dx, st_tok, st_cot):
    dma = pltpu.SemaphoreType.DMA

    def each(*shape):
        return [
            pltpu.VMEM((Q, *shape, PART), BF), pltpu.VMEM((1, *shape, META), BF), pltpu.VMEM((Q, *shape, PART), BF)
        ]

    held = (8, 2, ROWS)
    return pl.pallas_call(
        return_kernel,
        name="give_back",
        out_shape=(
            jax.ShapeDtypeStruct((TOK, HALF), BF),
            jax.ShapeDtypeStruct((TOK, HALF), BF),
            jax.ShapeDtypeStruct((TOP, TOK), F32),
        ),
        in_specs=[ANY] * 5,
        out_specs=[VMEM] * 3,
        scratch_shapes=[
            pltpu.VMEM((Q, *held, 2 * PART), BF), pltpu.VMEM((1, *held, META), BF), pltpu.VMEM((Q, *held, 2 * PART), BF),
            pltpu.VMEM((2, ALL, SPAN), BF), pltpu.VMEM((2, ALL, SPAN), BF),
            pltpu.VMEM((2, SPAN, ALL), BF), pltpu.VMEM((2, SPAN, ALL), BF),
            *each(2, 2, 4, TOK), *each(2, 2, TOK), *each(2, 4, TOK), *each(4, TOK), *each(4, TOK),
            dma((3, Q, 8)), dma((3, Q, 8)), dma((3, Q, 2)), dma((3, Q, 2)), dma((3, Q, 2)), dma((3, Q, 2)),
            dma((3, Q, 4)), dma((3, Q, 4)), dma((3, Q)), dma((2,)),
        ],
        compiler_params=pltpu.CompilerParams(
            collective_id=1, has_side_effects=True, vmem_limit_bytes=LIMIT
        ),
    )(y, ym, dx, st_tok, st_cot)


def hand_over_kernel(a, b, c, a_out, b_out, c_out):
    a_out[...] = a[...]
    b_out[...] = b[...]
    c_out[...] = c[...]


def hand_over(*values):
    return pl.pallas_call(
        hand_over_kernel,
        name="hand_over",
        out_shape=tuple(jax.ShapeDtypeStruct(v.shape, v.dtype) for v in values),
        in_specs=[VMEM] * 3,
        out_specs=[VMEM] * 3,
    )(*values)


def body(tokens, expert_ids, combine, cotangent, old_layout, pair_moves, gate_w, up_w, down_w):
    x, dy, st_tok, st_cot, wg_new, wu_new, wd_new, perm = dispatch(
        tokens, cotangent, expert_ids.T, combine.T, old_layout, pair_moves, gate_w, up_w, down_w
    )
    y_rows, y_meta, dx_rows, gg, gu, gd = experts(
        old_layout, pair_moves, x.reshape(2, ALL, WIDE), dy.reshape(2, ALL, D), perm,
        gate_w, up_w, down_w, wg_new, wu_new, wd_new,
    )
    mixed, d_tokens, d_combine = give_back(
        y_rows.reshape(Q, 2, 8, ROWS, 2 * PART), y_meta.reshape(1, 2, 8, ROWS, META),
        dx_rows.reshape(Q, 2, 8, ROWS, 2 * PART), st_tok, st_cot,
    )
    mixed, d_tokens, d_combine = hand_over(mixed, d_tokens, d_combine)
    return mixed, d_tokens, d_combine.T, gg, gu, gd


def solution(mesh):
    fine = Mesh(mesh.devices.reshape(2, 4, 4, 2, 2), (*EP, "xhi"))
    return jax.shard_map(
        body,
        mesh=fine,
        in_specs=(
            P(EP, None), P(EP, None), P(EP, None), P(EP, None), P(), P(),
            P(EP, None, "xhi"), P(EP, None, "xhi"), P(EP, "xhi", None),
        ),
        out_specs=(
            P(EP, "xhi"), P(EP, "xhi"), P(EP, None),
            P(EP, None, "xhi"), P(EP, None, "xhi"), P(EP, "xhi", None),
        ),
        check_vma=False,
    )
```
